32 devices in a mesh: dom: 8 (over z, x), tp: 4 (over y, core).
Axes of the slice: x: 2, y: 2, z: 4, core: 2. Of those that a mesh axis runs over, the one named last changes fastest.
Arguments:
- features: bfloat16 [32768, 512], P('dom'), may hold values from -6 to 6
- adjacency: bfloat16 [32768, 128], P('dom'), may hold values from -0.5 to 0.5
- node_mask: int32 [32768], P('dom'), may hold values 0 or 1
- mask_token: bfloat16 [512], replicated, may hold values from -6 to 6
- enc_weight: bfloat16 [512, 512], P(None, 'tp'), may hold values from -0.25 to 0.25
- enc_bias: bfloat16 [512], P('tp'), may hold values from -3 to 3
- gain: float32 [512], replicated, may hold values from -0.25 to 0.25
- requests: int32 [8, 8], P(None, 'dom'), may hold values from 0 to 31
- pair_first: int32 [8, 4, 64], P('dom', 'tp'), may hold values from 0 to 7
- pair_second: int32 [8, 4, 64], P('dom', 'tp'), may hold values from 0 to 9
- label_words: int32 [8, 4, 64, 8, 128], P('dom', 'tp'), may hold values from 0 to 65280
- pair_count: int32 [8, 4], P('dom', 'tp'), may hold values from 16 to 64, as said below
Outputs:
- weight_grad: float32 [512, 512], P(None, 'tp')
- bias_grad: float32 [512], P('tp')
- gain_grad: float32 [512], P('tp')
The draws below stay inside these ranges and needn't reach their ends.
Inputs may be any that keep to these rules, and one draw needn't show every extreme that they name: Every partition requests exactly one block from every partition, itself included. Slots p >= pair_count are padding; some device has all 64 slots live.
All inputs are finite; a program needn't handle non-finite values. No bound on the sum of `node_mask` on one device may be relied on, other than what follows from the above.
Results may differ from the reference program's by a relative error of at most 0.0018.
Values may be sent and summed in bfloat16 or wider, within the bound.
A program may use at most 128 MiB of HBM per device.

```python
import jax
import jax.numpy as jnp
from jax import lax

D = 512
BLK = 128
GROUP = 8
NB_DEV = 32
PAIRS_DEV = 64
NODES = 32768
N_DOM = 8
N_TP = 4


def draw_pair_count(key, part):
    first_key, second_key = jax.random.split(key)
    base = jax.random.randint(first_key, (N_DOM * N_TP,), PAIRS_DEV // 4, PAIRS_DEV + 1)
    where_full = jax.random.randint(second_key, (), 0, N_DOM * N_TP)
    filled = jnp.where(jnp.arange(N_DOM * N_TP) == where_full, PAIRS_DEV, base)
    return filled.reshape(N_DOM, N_TP).astype(jnp.int32)


def plant(array, rng, smallest, largest):
    longest = array.shape.index(max(array.shape))
    spots = []
    for shift in (0, 1):
        where = [jax.random.randint(jax.random.fold_in(rng, axis), (), 0, length) for axis, length in enumerate(array.shape)]
        where[longest] = (where[longest] + shift) % array.shape[longest]
        spots.append(tuple(where))
    return array.at[spots[0]].set(smallest).at[spots[1]].set(largest)


def block_scale(rng, dims, shards, low, high):
    level = 1.0
    for position, parts in shards:
        steps = jax.random.uniform(jax.random.fold_in(jax.random.fold_in(rng, 6), position), (parts,), jnp.float32, low / len(shards), high / len(shards))
        level = level * jnp.repeat(jnp.exp(steps), dims[position] // parts).reshape((-1,) + (1,) * (len(dims) - 1 - position))
    return level


def scatter_about(own_key, shape, spread, bound, cuts=(), kind=jnp.bfloat16):
    drawn = jax.random.normal(own_key, shape, jnp.float32) * spread
    if len(cuts) > 0:
        drawn = block_scale(own_key, shape, cuts, -0.22, 0.18) * drawn
    return jnp.clip(drawn, min=-bound, max=bound).astype(kind)


def setup_inputs(seed: int = 0) -> dict:
    streams_of = jax.random.split(jax.random.key(seed), 13)
    return {
        "features": scatter_about(streams_of[0], (NODES, D), 1.0, 6.0, ((0, 8),)),
        "adjacency": scatter_about(streams_of[1], (NODES, BLK), BLK ** -0.5, 0.5, ((0, 8),)),
        "node_mask": plant((jax.random.randint(streams_of[2], (NODES,), 0, 4) < 1).astype(jnp.int32), jax.random.fold_in(streams_of[2], 1), 0, 1),
        "mask_token": scatter_about(streams_of[3], (D,), 1.0, 6.0),
        "enc_weight": scatter_about(streams_of[4], (D, D), D ** -0.5, 0.25, ((1, 4),)),
        "enc_bias": scatter_about(streams_of[5], (D,), 0.5, 3.0, ((0, 4),)),
        "gain": scatter_about(streams_of[6], (D,), 0.06, 0.25, (), jnp.float32),
        "requests": plant(jax.random.randint(streams_of[7], (N_DOM, N_DOM), 0, NB_DEV), jax.random.fold_in(streams_of[7], 1), 0, NB_DEV - 1).astype(jnp.int32),
        "pair_first": plant(jax.random.randint(streams_of[8], (N_DOM, N_TP, PAIRS_DEV), 0, NB_DEV // N_TP), jax.random.fold_in(streams_of[8], 1), 0, (NB_DEV // N_TP) - 1).astype(jnp.int32),
        "pair_second": plant(jax.random.randint(streams_of[9], (N_DOM, N_TP, PAIRS_DEV), 0, NB_DEV // N_TP + N_DOM // N_TP), jax.random.fold_in(streams_of[9], 1), 0, (NB_DEV // N_TP + N_DOM // N_TP) - 1).astype(jnp.int32),
        "label_words": plant(jax.random.randint(streams_of[10], (N_DOM, N_TP, PAIRS_DEV, BLK // 16, BLK), 0, 65281), jax.random.fold_in(streams_of[10], 1), 0, 65280).astype(jnp.int32),
        "pair_count": draw_pair_count(jax.random.fold_in(streams_of[12], 71), 0),
    }


LOSS_NORM = 256.0


def silu_slope(value):
    sig = jax.nn.sigmoid(value)
    return sig * (1.0 + value * (1.0 - sig))


def unpack_labels(words):
    shifts = jnp.arange(16, dtype=jnp.int32)
    bits = jnp.bitwise_and(jnp.right_shift(words[:, :, None, :], shifts[None, None, :, None]), 1)
    return bits.reshape(words.shape[0], words.shape[1] * 16, words.shape[2]).astype(jnp.float32)


def decode(stack, local_count, first, second, words, count, gain):
    total = stack.shape[0]
    first_acc = jnp.zeros((local_count, stack.shape[1], stack.shape[2]), jnp.float32)
    second_acc = jnp.zeros((total, stack.shape[1], stack.shape[2]), jnp.float32)

    def step(carry, group):
        first_acc, second_acc = carry
        start = group * GROUP
        index_a = lax.dynamic_slice_in_dim(first, start, GROUP, 0)
        index_b = lax.dynamic_slice_in_dim(second, start, GROUP, 0)
        word_rows = lax.dynamic_slice_in_dim(words, start, GROUP, 0)
        tile_a = stack[index_a]
        tile_b = stack[index_b]
        scaled = (tile_a.astype(jnp.float32) * gain[None, None, :]).astype(jnp.bfloat16)
        logits = jnp.einsum("pif,pjf->pij", scaled.astype(jnp.float32), tile_b.astype(jnp.float32))
        live = ((start + jnp.arange(GROUP, dtype=jnp.int32)) < count).astype(jnp.float32)
        slope = ((jax.nn.sigmoid(logits) - unpack_labels(word_rows)) * live[:, None, None] / LOSS_NORM).astype(jnp.bfloat16)
        part_a = jnp.einsum("pij,pjf->pif", slope.astype(jnp.float32), tile_b.astype(jnp.float32))
        part_b = jnp.einsum("pij,pif->pjf", slope.astype(jnp.float32), scaled.astype(jnp.float32))
        return (first_acc.at[index_a].add(part_a), second_acc.at[index_b].add(part_b)), None

    groups = jnp.arange(first.shape[0] // GROUP, dtype=jnp.int32)
    (first_acc, second_acc), _ = lax.scan(step, (first_acc, second_acc), groups)
    return first_acc, second_acc


def reference(features, adjacency, node_mask, mask_token, enc_weight, enc_bias, gain, requests, pair_first, pair_second, label_words, pair_count):
    masked = jnp.where(node_mask[:, None] == 1, mask_token[None, :], features)
    blocks = masked.reshape(-1, BLK, D)
    mixed = jnp.einsum("bij,bjf->bif", adjacency.reshape(-1, BLK, BLK).astype(jnp.float32), blocks.astype(jnp.float32))
    agg = (blocks.astype(jnp.float32) + mixed).reshape(NODES, D).astype(jnp.bfloat16)
    pre = jnp.dot(agg, enc_weight, preferred_element_type=jnp.float32) + enc_bias.astype(jnp.float32)
    z_all = jax.nn.silu(pre).astype(jnp.bfloat16)
    z_blocks = z_all.reshape(N_DOM, NB_DEV, BLK, D)
    own_count = NB_DEV // N_TP
    source_count = N_DOM // N_TP
    grads = jnp.zeros((N_DOM, NB_DEV, BLK, D), jnp.float32)
    gain_total = jnp.zeros((D,), jnp.float32)

    def unit(carry, index):
        grads, gain_total = carry
        part = index // N_TP
        lane = index % N_TP
        mine = lax.dynamic_index_in_dim(z_blocks, part, 0, keepdims=False)
        own_ids = (lane * own_count + jnp.arange(own_count, dtype=jnp.int32)).astype(jnp.int32)
        local = mine[own_ids]
        sources = (lane * source_count + jnp.arange(source_count, dtype=jnp.int32)).astype(jnp.int32)
        wanted = lax.dynamic_index_in_dim(requests, part, 0, keepdims=False)[sources]
        remote = z_blocks[sources, wanted]
        stack = jnp.concatenate([local, remote], axis=0)
        first_acc, second_acc = decode(stack, own_count, pair_first[part, lane], pair_second[part, lane], label_words[part, lane], pair_count[part, lane], gain)
        local_grad = gain[None, None, :] * first_acc + second_acc[:own_count]
        grads = grads.at[part, own_ids].add(local_grad)
        grads = grads.at[sources, wanted].add(second_acc[own_count:])
        gain_total = gain_total + jnp.sum(local.astype(jnp.float32) * first_acc, axis=(0, 1))
        return (grads, gain_total), None

    (grads, gain_total), _ = lax.scan(unit, (grads, gain_total), jnp.arange(N_DOM * N_TP, dtype=jnp.int32))
    dpre = grads.reshape(NODES, D) * silu_slope(pre)
    weight_grad = jnp.dot(agg.T, dpre.astype(jnp.bfloat16), preferred_element_type=jnp.float32)
    bias_grad = jnp.sum(dpre, axis=0)
    return (weight_grad, bias_grad, gain_total)
```

```python
import functools

import jax
import jax.numpy as jnp
from jax import lax
from jax.experimental import pallas as pl
from jax.experimental.pallas import tpu as pltpu
from jax.sharding import PartitionSpec as P

NORM = 256.0
WORD = 16
EXTRA = 8
MESH = pl.DeviceIdType.MESH
LIMIT = 60 * 1024 * 1024
f32 = jnp.float32
bf16 = jnp.bfloat16


def served(lane):
    return lax.rem(lane, 2) * 2 + lax.div(lane, 2)


def slope_tile(half_logits, ones, live):
    sig = 0.5 * jnp.tanh(half_logits) + 0.5
    clear = sig.astype(bf16).astype(f32)
    marked = (sig - 1.0).astype(bf16).astype(f32)
    return (live * clear + ones * (marked - clear)).astype(bf16)


def rows_of(k, block, many=1):
    start = k * block
    if not isinstance(start, int):
        start = pl.multiple_of(start, block)
    return pl.ds(start, many * block)


def step_kernel(
    cfg, requests, feat_hbm, adj_hbm, mask_hbm, token_hbm, weight_hbm, bias_hbm, gain_hbm,
    first_hbm, second_hbm, count_hbm, words_hbm,
    result,
    feat, adj, mask, token, bias, gain, first, second, count, words,
    gathered, packed, asked, landed, agg, z, scaled, curve, ones, live, slope, first_acc, second_acc, dpre,
    part, recv_core, sum_core, recv_y, total, recv_x, half, recv_z, recv_small, far_bias,
    feat_sem, w_send, w_recv, a_send, a_recv, core_send, core_recv, y_send, y_recv, x_send, x_recv,
    z_send, z_recv, gz_send, gz_recv, gx_send, gx_recv, small_send, small_recv,
):
    doms, own, wanted, chunks = cfg
    depth = doms // 2
    d = lax.axis_index("dom")
    t = lax.axis_index("tp")
    low = lax.rem(t, 2)
    high = lax.div(t, 2)
    core_peer = high * 2 + (1 - low)
    y_peer = (1 - high) * 2 + low
    xi = lax.rem(d, 2)
    zi = lax.div(d, 2)
    x_peer = zi * 2 + (1 - xi)
    a = lax.div(d, wanted)
    j = lax.rem(d, wanted)
    width, quarter = weight_hbm.shape
    block = mask.shape[2]

    def z_peer(o):
        return lax.rem(zi + o, depth) * 2 + xi

    pairs = (
        (weight_hbm, packed.at[pl.ds(0, width)]), (bias_hbm, bias), (token_hbm, token), (mask_hbm, mask),
        (adj_hbm, adj), (feat_hbm, feat), (gain_hbm, gain), (first_hbm, first), (second_hbm, second),
        (count_hbm, count), (words_hbm, words),
    )
    fetches = [pltpu.make_async_copy(source, target, feat_sem.at[k]) for k, (source, target) in enumerate(pairs)]
    for fetch in fetches:
        fetch.start()

    barrier = pltpu.get_barrier_semaphore()

    def greet(peer):
        pl.semaphore_signal(barrier, inc=1, device_id=peer, device_id_type=MESH)

    greet({"tp": core_peer})
    greet({"tp": y_peer})

    @pl.loop(1, doms)
    def _(o):
        greet({"dom": lax.rem(d + o, doms)})

    def pair_of(c):
        return served(t) * wanted + lax.rem(j + c, wanted), a

    alone = jnp.logical_and(a == t, served(t) == t)
    for c in range(wanted):
        target = pair_of(c)
        source = t * wanted + lax.rem(j - c + wanted, wanted), served(a)

        def both(target=target, source=source):
            greet(target)
            greet(source)

        if c == 0:
            pl.when(jnp.logical_not(alone))(both)
        else:
            both()

    columns = lambda c: pl.ds(pl.multiple_of(c * quarter, quarter), quarter)
    fetches[0].wait()
    fetches[1].wait()
    packed[pl.ds(width, 16), :] = jnp.broadcast_to(bias[...], (16, quarter))
    gathered[:, columns(t)] = packed[...]
    pl.semaphore_wait(barrier, 2 + doms - 1 + 2 * wanted - jnp.where(alone, 2, 0))

    def weight_copy(k, source, column, peer):
        return pltpu.make_async_remote_copy(
            src_ref=source, dst_ref=gathered.at[:, columns(column)],
            send_sem=w_send.at[k], recv_sem=w_recv.at[k],
            device_id={"tp": peer}, device_id_type=MESH,
        )

    across = weight_copy(0, packed, t, y_peer)
    near = weight_copy(1, packed, t, core_peer)
    relay = weight_copy(2, gathered.at[:, columns(y_peer)], y_peer, core_peer)
    across.start()
    near.start()

    rows = lax.broadcasted_iota(jnp.int32, (block, block), 0)
    cols = lax.broadcasted_iota(jnp.int32, (block, block), 1)
    for fetch in fetches[2:]:
        fetch.wait()
    token32 = token[...].astype(f32)
    token_row = jnp.concatenate([token32[k : k + 1, :] for k in range(token32.shape[0])], axis=1)

    def aggregate(node_block):
        hidden = jnp.sum(jnp.where(rows == cols, mask[node_block].astype(f32), 0.0), axis=1, keepdims=True)
        masked32 = jnp.where(hidden == 1.0, token_row, feat[node_block].astype(f32))
        mixed = jnp.dot(adj[node_block], masked32.astype(bf16), preferred_element_type=f32)
        return (masked32 + mixed).astype(bf16)

    for k in range(wanted):
        asked[k] = aggregate(requests[served(t) * wanted + k])

    def agg_copy(c):
        return pltpu.make_async_remote_copy(
            src_ref=asked.at[lax.rem(j + c, wanted)], dst_ref=landed.at[j],
            send_sem=a_send.at[c], recv_sem=a_recv.at[c],
            device_id=pair_of(c), device_id_type=MESH,
        )

    pl.when(jnp.logical_not(alone))(lambda: agg_copy(0).start())
    for c in range(1, wanted):
        agg_copy(c).start()

    @pl.when(alone)
    def _():
        landed[j] = asked[j]

    for k in range(own):
        agg[rows_of(k, block), :] = aggregate(t * own + k)

    slots = first.shape[1]
    cells = own * (own + wanted)
    key = second[...] * own + first[...]
    cell = lax.broadcasted_iota(jnp.int32, (cells, slots), 0)
    slot = lax.broadcasted_iota(jnp.int32, (cells, slots), 1)
    hot32 = jnp.where(jnp.logical_and(cell == key, slot < count[...]), 1.0, 0.0)
    live[...] = jnp.broadcast_to(jnp.sum(hot32, axis=1, keepdims=True), (cells, block))
    hot = hot32.astype(bf16)

    def count_labels(w):
        word = words[pl.ds(w, slots, stride=block // WORD), :]
        for b in range(0, WORD, 2):
            bits = jnp.concatenate(
                [jnp.bitwise_and(jnp.right_shift(word, b + q), 1).astype(f32).astype(bf16) for q in range(2)], axis=1
            )
            counts = jnp.dot(hot, bits, preferred_element_type=f32)
            for q in range(2):
                for ib in range(own + wanted):
                    ones[ib, pl.ds(w * WORD + b + q, own, stride=block), :] = counts[
                        ib * own : (ib + 1) * own, q * block : (q + 1) * block
                    ]

    early = block // WORD // 2
    pl.loop(0, early)(count_labels)
    across.wait_recv()
    relay.start()
    pl.loop(early, block // WORD)(count_labels)
    near.wait_recv()
    relay.wait_recv()

    matrix = gathered[:width, :]
    shift = gathered[width : width + 1, :].astype(f32)
    half_gain = 0.5 * gain[...]

    def activate(k):
        spot = rows_of(k, block, 2)
        pre = jnp.dot(agg[spot, :], matrix, preferred_element_type=f32) + shift
        sig = 0.5 * jnp.tanh(0.5 * pre) + 0.5
        curve[spot, :] = sig * (1.0 + pre * (1.0 - sig)) * (2.0 / NORM)
        value = (pre * sig).astype(bf16)
        z[spot, :] = value
        return value

    for k in range(0, own, 2):
        value = activate(k)
        scaled[rows_of(k, block, 2), :] = (value.astype(f32) * half_gain).astype(bf16)

    def score(k, ib):
        logits = lax.dot_general(
            scaled[rows_of(k, block, 2), :], z[rows_of(ib, block, 2), :], (((1,), (1,)), ((), ())),
            preferred_element_type=f32,
        )
        for q in range(2):
            for r in range(2):
                slope[rows_of(k + q, block), rows_of(ib + r, block)] = slope_tile(
                    logits[q * block : (q + 1) * block, r * block : (r + 1) * block],
                    ones[ib + r, rows_of(k + q, block), :],
                    live[pl.ds((ib + r) * own + k + q, 1), :],
                )

    mine = pl.ds(0, own * block)
    for k in range(0, own, 2):
        for ib in range(0, own, 2):
            score(k, ib)
        first_acc[rows_of(k, block, 2), :] = jnp.dot(
            slope[rows_of(k, block, 2), mine], z[mine, :], preferred_element_type=f32
        )

    def second_of(ib):
        return lax.dot_general(
            slope[:, rows_of(ib, block, 2)], scaled[...], (((0,), (0,)), ((), ())), preferred_element_type=f32
        )

    for ib in range(0, own, 2):
        second_acc[rows_of(ib, block, 2), :] = second_of(ib)

    pl.when(jnp.logical_not(alone))(lambda: agg_copy(0).wait())
    for c in range(1, wanted):
        agg_copy(c).wait()
    across.wait_send()
    near.wait_send()
    relay.wait_send()

    far_bias[...] = jnp.zeros_like(far_bias)

    @pl.loop(0, wanted // 2)
    def _(step):
        ib = own + 2 * step
        spot = rows_of(ib, block, 2)
        agg[spot, :] = landed[pl.ds(2 * step, 2)].reshape(2 * block, width)
        value = activate(ib)
        for k in range(0, own, 2):
            score(k, ib)
            first_acc[rows_of(k, block, 2), :] += jnp.dot(
                slope[rows_of(k, block, 2), spot], value, preferred_element_type=f32
            )
        change = second_of(ib) * curve[spot, :]
        dpre[spot, :] = change.astype(bf16)
        far_bias[...] += jnp.sum(change, axis=0, keepdims=True)

    lanes = width // quarter
    bias_sum = far_bias[...]
    gain_sum = jnp.zeros((1, width), f32)
    for k in range(0, own, 2):
        spot = rows_of(k, block, 2)
        value = first_acc[spot, :]
        gain_sum += jnp.sum(z[spot, :].astype(f32) * value, axis=0, keepdims=True)
        value = (half_gain * value + second_acc[spot, :]) * curve[spot, :]
        bias_sum += jnp.sum(value, axis=0, keepdims=True)
        dpre[spot, :] = value.astype(bf16)
    gain_sum = gain_sum * (1.0 / NORM)
    row = lax.broadcasted_iota(jnp.int32, (EXTRA, width), 0)
    extra = jnp.where(row == 0, bias_sum, jnp.where(row == 1, gain_sum, 0.0))
    for c in range(lanes):
        part[c, pl.ds(0, EXTRA), :] = extra[:, c * quarter : (c + 1) * quarter]

    tall = width // chunks
    side = tall // 2
    piece = side // depth

    def chunk_rows(c):
        return pl.ds(0, EXTRA + tall) if c == 0 else pl.ds(EXTRA + c * tall, tall)

    def core_copy(c, h):
        return pltpu.make_async_remote_copy(
            src_ref=part.at[2 * h + 1 - low, chunk_rows(c)], dst_ref=recv_core.at[h, chunk_rows(c)],
            send_sem=core_send.at[c, h], recv_sem=core_recv.at[c, h],
            device_id={"tp": core_peer}, device_id_type=MESH,
        )

    def y_copy(c):
        return pltpu.make_async_remote_copy(
            src_ref=sum_core.at[chunk_rows(c)], dst_ref=recv_y.at[chunk_rows(c)],
            send_sem=y_send.at[c], recv_sem=y_recv.at[c],
            device_id={"tp": y_peer}, device_id_type=MESH,
        )

    def side_rows(c, x):
        return pl.ds(pl.multiple_of(EXTRA + c * tall + x * side, 8), side)

    def piece_rows(c, x, p):
        return pl.ds(pl.multiple_of(EXTRA + c * tall + x * side + p * piece, 8), piece)

    def x_copy(c):
        return pltpu.make_async_remote_copy(
            src_ref=total.at[side_rows(c, 1 - xi)], dst_ref=recv_x.at[c],
            send_sem=x_send.at[c], recv_sem=x_recv.at[c],
            device_id={"dom": x_peer}, device_id_type=MESH,
        )

    def z_copy(c, o):
        p = lax.rem(zi + o, depth)
        return pltpu.make_async_remote_copy(
            src_ref=half.at[c, pl.ds(pl.multiple_of(p * piece, 8), piece)], dst_ref=recv_z.at[c, o],
            send_sem=z_send.at[c, o], recv_sem=z_recv.at[c, o],
            device_id={"dom": z_peer(o)}, device_id_type=MESH,
        )

    def gz_copy(c, o):
        here = piece_rows(c, xi, zi)
        return pltpu.make_async_remote_copy(
            src_ref=result.at[here], dst_ref=result.at[here],
            send_sem=gz_send.at[c, o], recv_sem=gz_recv.at[c, o],
            device_id={"dom": z_peer(o)}, device_id_type=MESH,
        )

    def gx_copy(c):
        here = side_rows(c, xi)
        return pltpu.make_async_remote_copy(
            src_ref=result.at[here], dst_ref=result.at[here],
            send_sem=gx_send.at[c], recv_sem=gx_recv.at[c],
            device_id={"dom": x_peer}, device_id_type=MESH,
        )

    def small_copy(o):
        return pltpu.make_async_remote_copy(
            src_ref=total.at[pl.ds(0, EXTRA)], dst_ref=recv_small.at[d],
            send_sem=small_send.at[o], recv_sem=small_recv.at[o],
            device_id={"dom": lax.rem(d + o, doms)}, device_id_type=MESH,
        )

    wide = 2 if chunks > 1 else 1
    for c in range(0, chunks, wide):
        both = lax.dot_general(
            agg[:, pl.ds(c * tall, wide * tall)], dpre[...], (((0,), (0,)), ((), ())), preferred_element_type=f32
        )
        for q in range(lanes):
            part[q, pl.ds(EXTRA + c * tall, wide * tall), :] = both[:, q * quarter : (q + 1) * quarter]
        for e in range(c, c + wide):
            core_copy(e, 1 - high).start()
            core_copy(e, high).start()

    def to_y(c):
        core_copy(c, 1 - high).wait_recv()
        spot = chunk_rows(c)
        sum_core[spot, :] = part[2 * (1 - high) + low, spot, :] + recv_core[1 - high, spot, :]
        y_copy(c).start()

    def to_x(c):
        core_copy(c, high).wait_recv()
        y_copy(c).wait_recv()
        spot = chunk_rows(c)
        total[spot, :] = part[2 * high + low, spot, :] + recv_core[high, spot, :] + recv_y[spot, :]
        x_copy(c).start()

    def to_z(c):
        x_copy(c).wait_recv()
        half[c] = total[side_rows(c, xi), :] + recv_x[c]

        @pl.loop(1, depth)
        def _(o):
            z_copy(c, o).start()

    def back_z(c):
        @pl.loop(1, depth)
        def _(o):
            z_copy(c, o).wait_recv()

        sums = half[c, pl.ds(pl.multiple_of(zi * piece, 8), piece), :]
        for o in range(1, depth):
            sums += recv_z[c, o]
        result[piece_rows(c, xi, zi), :] = sums

        @pl.loop(1, depth)
        def _(o):
            gz_copy(c, o).start()

    def back_x(c):
        @pl.loop(1, depth)
        def _(o):
            gz_copy(c, o).wait_recv()

        gx_copy(c).start()

    for c in range(chunks):
        to_y(c)
    stages = (to_x, to_z, back_z, back_x)
    for step in range(chunks + len(stages) - 1):
        for k, stage in enumerate(stages):
            if 0 <= step - k < chunks:
                stage(step - k)
        if step == 0:
            recv_small[d] = total[pl.ds(0, EXTRA), :]

            @pl.loop(1, doms)
            def _(o):
                small_copy(o).start()

    @pl.loop(1, doms)
    def _(o):
        small_copy(o).wait()

    sums = recv_small[0]
    for k in range(1, doms):
        sums += recv_small[k]
    result[pl.ds(0, EXTRA), :] = sums

    for c in range(chunks):
        core_copy(c, 0).wait_send()
        core_copy(c, 1).wait_send()
        y_copy(c).wait_send()
        x_copy(c).wait_send()

        @pl.loop(1, depth)
        def _(o):
            z_copy(c, o).wait_send()
            gz_copy(c, o).wait_send()

        gx_copy(c).wait()


def step(cfg, requests, feat, adj, mask, token, weight, bias, gain, first, second, count, words):
    doms, own, wanted, chunks = cfg
    nblocks, block, width = feat.shape
    quarter = weight.shape[1]
    lanes = width // quarter
    total = own + wanted
    depth = doms // 2
    tall = width // chunks
    high = EXTRA + width
    dma = pltpu.SemaphoreType.DMA
    anywhere = pl.BlockSpec(memory_space=pltpu.HBM)
    return pl.pallas_call(
        functools.partial(step_kernel, cfg),
        in_specs=[pl.BlockSpec(memory_space=pltpu.SMEM)] + [anywhere] * 11,
        out_specs=pl.BlockSpec(memory_space=pltpu.VMEM),
        out_shape=jax.ShapeDtypeStruct((high, quarter), f32),
        scratch_shapes=[
            pltpu.VMEM(feat.shape, bf16),
            pltpu.VMEM(adj.shape, bf16),
            pltpu.VMEM(mask.shape, jnp.int32),
            pltpu.VMEM(token.shape, bf16),
            pltpu.VMEM(bias.shape, bf16),
            pltpu.VMEM(gain.shape, f32),
            pltpu.VMEM(first.shape, jnp.int32),
            pltpu.VMEM(second.shape, jnp.int32),
            pltpu.VMEM(count.shape, jnp.int32),
            pltpu.VMEM(words.shape, jnp.int32),
            pltpu.VMEM((width + 16, width), bf16),
            pltpu.VMEM((width + 16, quarter), bf16),
            pltpu.VMEM((wanted, block, width), bf16),
            pltpu.VMEM((wanted, block, width), bf16),
            pltpu.VMEM((total * block, width), bf16),
            pltpu.VMEM((total * block, width), bf16),
            pltpu.VMEM((own * block, width), bf16),
            pltpu.VMEM((total * block, width), f32),
            pltpu.VMEM((total, own * block, block), f32),
            pltpu.VMEM((total * own, block), f32),
            pltpu.VMEM((own * block, total * block), bf16),
            pltpu.VMEM((own * block, width), f32),
            pltpu.VMEM((own * block, width), f32),
            pltpu.VMEM((total * block, width), bf16),
            pltpu.VMEM((lanes, high, quarter), f32),
            pltpu.VMEM((2, high, quarter), f32),
            pltpu.VMEM((high, quarter), f32),
            pltpu.VMEM((high, quarter), f32),
            pltpu.VMEM((high, quarter), f32),
            pltpu.VMEM((chunks, tall // 2, quarter), f32),
            pltpu.VMEM((chunks, tall // 2, quarter), f32),
            pltpu.VMEM((chunks, depth, tall // 2 // depth, quarter), f32),
            pltpu.VMEM((doms, EXTRA, quarter), f32),
            pltpu.VMEM((1, width), f32),
            dma((11,)), dma((3,)), dma((3,)), dma((wanted,)), dma((wanted,)),
            dma((chunks, 2)), dma((chunks, 2)), dma((chunks,)), dma((chunks,)), dma((chunks,)), dma((chunks,)),
            dma((chunks, depth)), dma((chunks, depth)), dma((chunks, depth)), dma((chunks, depth)),
            dma((chunks,)), dma((chunks,)), dma((doms,)), dma((doms,)),
        ],
        compiler_params=pltpu.CompilerParams(collective_id=0, has_side_effects=True, vmem_limit_bytes=LIMIT),
    )(requests, feat, adj, mask, token, weight, bias, gain, first, second, count, words)


def body(
    features, adjacency, node_mask, mask_token, enc_weight, enc_bias, gain, requests,
    pair_first, pair_second, label_words, pair_count,
):
    nodes, width = features.shape
    block = adjacency.shape[1]
    nblocks = nodes // block
    doms = lax.axis_size("dom")
    lanes = lax.axis_size("tp")
    slots = pair_first.shape[2]
    chunks = min(4, width // (doms * 8))
    cfg = doms, nblocks // lanes, doms // lanes, chunks
    result = step(
        cfg, requests.reshape(doms),
        features.reshape(nblocks, block, width),
        adjacency.reshape(nblocks, block, block),
        node_mask.reshape(nblocks, 1, block),
        mask_token.reshape(width // 128, 128), enc_weight, enc_bias.reshape(1, -1), gain.reshape(1, width),
        pair_first.reshape(1, slots), pair_second.reshape(1, slots), pair_count.reshape(1, 1),
        label_words.reshape(slots * label_words.shape[3], block),
    )
    return result[EXTRA:], result[0], result[1]


def solution(mesh):
    placed = (
        P("dom", None),
        P("dom", None),
        P("dom"),
        P(),
        P(None, "tp"),
        P("tp"),
        P(),
        P(None, "dom"),
        P("dom", "tp", None),
        P("dom", "tp", None),
        P("dom", "tp", None, None, None),
        P("dom", "tp"),
    )
    return jax.shard_map(
        body,
        mesh=mesh,
        in_specs=placed,
        out_specs=(P(None, "tp"), P("tp"), P("tp")),
        check_vma=False,
    )
```

```python
import functools

import jax
import jax.numpy as jnp
from jax import lax
from jax.experimental import pallas as pl
from jax.experimental.pallas import tpu as pltpu
from jax.sharding import PartitionSpec as P

NORM = 256.0
WORD = 16
EXTRA = 8
MESH = pl.DeviceIdType.MESH
LIMIT = 60 * 1024 * 1024
f32 = jnp.float32
bf16 = jnp.bfloat16


def served(lane):
    return lax.rem(lane, 2) * 2 + lax.div(lane, 2)


def slope_tile(half_logits, ones, live):
    sig = 0.5 * jnp.tanh(half_logits) + 0.5
    clear = sig.astype(bf16).astype(f32)
    marked = (sig - 1.0).astype(bf16).astype(f32)
    return (live * clear + ones * (marked - clear)).astype(bf16)


def rows_of(k, block, many=1):
    start = k * block
    if not isinstance(start, int):
        start = pl.multiple_of(start, block)
    return pl.ds(start, many * block)


def step_kernel(
    cfg, requests, feat_hbm, adj_hbm, mask_hbm, token_hbm, weight_hbm, bias_hbm, gain_hbm,
    first_hbm, second_hbm, count_hbm, words_hbm,
    weight_out, bias_out, gain_out,
    feat, adj, mask, token, bias, gain, first, second, count, words,
    gathered, packed, asked, landed, agg, z, scaled, curve, ones, live, slope, first_acc, second_acc, dpre,
    part, recv_core, send_y, arrive_y, send_x, arrive_x, half, recv_z, far_bias, extras,
    feat_sem, w_send, w_recv, a_send, a_recv, core_send, core_recv, y_send, y_recv, x_send, x_recv,
    z_send, z_recv, g_send, g_recv,
):
    doms, own, wanted, lanes, slot_count = cfg
    depth = doms // 2
    d = lax.axis_index("dom")
    t = lax.axis_index("tp")
    low = lax.rem(t, 2)
    high = lax.div(t, 2)
    core_peer = high * 2 + (1 - low)
    y_peer = (1 - high) * 2 + low
    xi = lax.rem(d, 2)
    zi = lax.div(d, 2)
    x_peer = zi * 2 + (1 - xi)
    a = lax.div(d, wanted)
    j = lax.rem(d, wanted)
    width, quarter = weight_hbm.shape
    block = mask.shape[2]

    def z_peer(o):
        return lax.rem(zi + o, depth) * 2 + xi

    pairs = (
        (weight_hbm, packed.at[pl.ds(0, width)]), (bias_hbm, bias), (token_hbm, token), (mask_hbm, mask),
        (adj_hbm, adj), (feat_hbm, feat), (gain_hbm, gain), (first_hbm, first), (second_hbm, second),
        (count_hbm, count), (words_hbm, words),
    )
    fetches = [pltpu.make_async_copy(source, target, feat_sem.at[k]) for k, (source, target) in enumerate(pairs)]
    for fetch in fetches:
        fetch.start()

    barrier = pltpu.get_barrier_semaphore()

    def greet(peer):
        pl.semaphore_signal(barrier, inc=1, device_id=peer, device_id_type=MESH)

    greet({"tp": core_peer})
    greet({"tp": y_peer})

    @pl.loop(1, doms)
    def _(o):
        greet({"dom": lax.rem(d + o, doms)})

    greet((x_peer, y_peer))

    if slot_count == 3:
        home = high == lax.div(zi, 2)
        near_z = 2 * lax.div(zi, 2) + low
        far_z = 2 * (1 - lax.div(zi, 2)) + low
        outgoing = (
            (None, far_z * 2 + jnp.where(home, xi, 1 - xi)),
            (home, near_z * 2 + xi),
            (home, near_z * 2 + 1 - xi),
        )
        mine_slot = 1
        alone = zi == t

        def lane_from(jj):
            same_half = lax.div(zi, 2) == high
            straight = jnp.logical_or(same_half, xi == jj)
            return jnp.where(straight, high, 1 - high) * 2 + lax.rem(zi, 2)

        sends = 1 + jnp.where(home, 2, 0)
    else:
        outgoing = tuple((None, served(t) * wanted + lax.rem(j + c, wanted)) for c in range(wanted))
        mine_slot = 0
        alone = jnp.logical_and(a == t, served(t) == t)

        def lane_from(jj):
            return served(a)

        sends = wanted

    def when_sent(c, do):
        active = outgoing[c][0]
        if c == mine_slot:
            other = jnp.logical_not(alone)
            active = other if active is None else jnp.logical_and(active, other)
        if active is None:
            do()
        else:
            pl.when(active)(do)

    def when_from(jj, do):
        pl.when(jnp.logical_not(jnp.logical_and(alone, j == jj)))(do)

    for c in range(slot_count):
        when_sent(c, functools.partial(greet, (outgoing[c][1], a)))
    for jj in range(wanted):
        when_from(jj, functools.partial(greet, (t * wanted + jj, lane_from(jj))))

    columns = lambda c: pl.ds(pl.multiple_of(c * quarter, quarter), quarter)
    fetches[0].wait()
    fetches[1].wait()
    packed[pl.ds(width, 16), :] = jnp.broadcast_to(bias[...], (16, quarter))
    gathered[:, columns(t)] = packed[...]
    pl.semaphore_wait(barrier, 2 + doms + wanted + sends - jnp.where(alone, 2, 0))

    def weight_copy(k, source, column, peer):
        return pltpu.make_async_remote_copy(
            src_ref=source, dst_ref=gathered.at[:, columns(column)],
            send_sem=w_send.at[k], recv_sem=w_recv.at[k],
            device_id={"tp": peer}, device_id_type=MESH,
        )

    across = weight_copy(0, packed, t, y_peer)
    near = weight_copy(1, packed, t, core_peer)
    relay = weight_copy(2, gathered.at[:, columns(y_peer)], y_peer, core_peer)
    across.start()
    near.start()

    rows = lax.broadcasted_iota(jnp.int32, (block, block), 0)
    cols = lax.broadcasted_iota(jnp.int32, (block, block), 1)
    for fetch in fetches[2:]:
        fetch.wait()
    token32 = token[...].astype(f32)
    token_row = jnp.concatenate([token32[k : k + 1, :] for k in range(token32.shape[0])], axis=1)

    def aggregate(node_block):
        hidden = jnp.sum(jnp.where(rows == cols, mask[node_block].astype(f32), 0.0), axis=1, keepdims=True)
        masked32 = jnp.where(hidden == 1.0, token_row, feat[node_block].astype(f32))
        mixed = jnp.dot(adj[node_block], masked32.astype(bf16), preferred_element_type=f32)
        return (masked32 + mixed).astype(bf16)

    def agg_copy(c, slot):
        return pltpu.make_async_remote_copy(
            src_ref=asked.at[c], dst_ref=landed.at[slot],
            send_sem=a_send.at[c], recv_sem=a_recv.at[slot],
            device_id=(outgoing[c][1], a), device_id_type=MESH,
        )

    for c in range(slot_count):
        asked[c] = aggregate(requests[outgoing[c][1]])
        when_sent(c, lambda c=c: agg_copy(c, j).start())

    @pl.when(alone)
    def _():
        landed[j] = asked[mine_slot]

    for k in range(own):
        agg[rows_of(k, block), :] = aggregate(t * own + k)

    slots = first.shape[1]
    cells = own * (own + wanted)
    key = second[...] * own + first[...]
    cell = lax.broadcasted_iota(jnp.int32, (cells, slots), 0)
    slot = lax.broadcasted_iota(jnp.int32, (cells, slots), 1)
    hot32 = jnp.where(jnp.logical_and(cell == key, slot < count[...]), 1.0, 0.0)
    live[...] = jnp.broadcast_to(jnp.sum(hot32, axis=1, keepdims=True), (cells, block))
    hot = hot32.astype(bf16)

    def count_labels(w):
        word = words[pl.ds(w, slots, stride=block // WORD), :]
        for b in range(0, WORD, 2):
            bits = jnp.concatenate(
                [jnp.bitwise_and(jnp.right_shift(word, b + q), 1).astype(f32).astype(bf16) for q in range(2)], axis=1
            )
            counts = jnp.dot(hot, bits, preferred_element_type=f32)
            for q in range(2):
                for ib in range(own + wanted):
                    ones[ib, pl.ds(w * WORD + b + q, own, stride=block), :] = counts[
                        ib * own : (ib + 1) * own, q * block : (q + 1) * block
                    ]

    early = block // WORD // 2
    pl.loop(0, early)(count_labels)
    across.wait_recv()
    relay.start()
    pl.loop(early, block // WORD)(count_labels)
    near.wait_recv()
    relay.wait_recv()

    matrix = gathered[:width, :]
    shift = gathered[width : width + 1, :].astype(f32)
    half_gain = 0.5 * gain[...]

    def activate(k):
        spot = rows_of(k, block, 2)
        pre = jnp.dot(agg[spot, :], matrix, preferred_element_type=f32) + shift
        sig = 0.5 * jnp.tanh(0.5 * pre) + 0.5
        curve[spot, :] = sig * (1.0 + pre * (1.0 - sig)) * (2.0 / NORM)
        value = (pre * sig).astype(bf16)
        z[spot, :] = value
        return value

    for k in range(0, own, 2):
        value = activate(k)
        scaled[rows_of(k, block, 2), :] = (value.astype(f32) * half_gain).astype(bf16)

    def score(k, ib):
        logits = lax.dot_general(
            scaled[rows_of(k, block, 2), :], z[rows_of(ib, block, 2), :], (((1,), (1,)), ((), ())),
            preferred_element_type=f32,
        )
        for q in range(2):
            for r in range(2):
                slope[rows_of(k + q, block), rows_of(ib + r, block)] = slope_tile(
                    logits[q * block : (q + 1) * block, r * block : (r + 1) * block],
                    ones[ib + r, rows_of(k + q, block), :],
                    live[pl.ds((ib + r) * own + k + q, 1), :],
                )

    mine = pl.ds(0, own * block)
    for k in range(0, own, 2):
        for ib in range(0, own, 2):
            score(k, ib)
        first_acc[rows_of(k, block, 2), :] = jnp.dot(
            slope[rows_of(k, block, 2), mine], z[mine, :], preferred_element_type=f32
        )

    def second_of(ib):
        return lax.dot_general(
            slope[:, rows_of(ib, block, 2)], scaled[...], (((0,), (0,)), ((), ())), preferred_element_type=f32
        )

    for ib in range(0, own, 2):
        second_acc[rows_of(ib, block, 2), :] = second_of(ib)

    for jj in range(wanted):
        when_from(jj, lambda jj=jj: agg_copy(0, jj).wait_recv())
    for c in range(slot_count):
        when_sent(c, lambda c=c: agg_copy(c, j).wait_send())
    across.wait_send()
    near.wait_send()
    relay.wait_send()

    far_bias[...] = jnp.zeros_like(far_bias)

    @pl.loop(0, wanted // 2)
    def _(step):
        ib = own + 2 * step
        spot = rows_of(ib, block, 2)
        agg[spot, :] = landed[pl.ds(2 * step, 2)].reshape(2 * block, width)
        value = activate(ib)
        for k in range(0, own, 2):
            score(k, ib)
            first_acc[rows_of(k, block, 2), :] += jnp.dot(
                slope[rows_of(k, block, 2), spot], value, preferred_element_type=f32
            )
        change = second_of(ib) * curve[spot, :]
        dpre[spot, :] = change.astype(bf16)
        far_bias[...] += jnp.sum(change, axis=0, keepdims=True)

    bias_sum = far_bias[...]
    gain_sum = jnp.zeros((1, width), f32)
    for k in range(0, own, 2):
        spot = rows_of(k, block, 2)
        value = first_acc[spot, :]
        gain_sum += jnp.sum(z[spot, :].astype(f32) * value, axis=0, keepdims=True)
        value = (half_gain * value + second_acc[spot, :]) * curve[spot, :]
        bias_sum += jnp.sum(value, axis=0, keepdims=True)
        dpre[spot, :] = value.astype(bf16)
    gain_sum = gain_sum * (1.0 / NORM)
    row = lax.broadcasted_iota(jnp.int32, (EXTRA, width), 0)
    extra = jnp.where(row == 0, bias_sum, jnp.where(row == 1, gain_sum, 0.0))
    extras[...] = extra

    side = width // 2
    piece = side // depth

    def remote(source, target, send, recv, peer):
        return pltpu.make_async_remote_copy(
            src_ref=source, dst_ref=target, send_sem=send, recv_sem=recv, device_id=peer, device_id_type=MESH
        )

    def core_copy(h):
        return remote(part.at[h, 1 - low], recv_core.at[h], core_send.at[h], core_recv.at[h], {"tp": core_peer})

    across_peers = (d, y_peer), (x_peer, y_peer)

    def y_copy(k):
        return remote(send_y.at[k], arrive_y.at[k], y_send.at[k], y_recv.at[k], across_peers[k])

    def x_copy():
        return remote(send_x, arrive_x, x_send, x_recv, (x_peer, t))

    def z_copy(o):
        p = lax.rem(zi + o, depth)
        return remote(half.at[p], recv_z.at[o], z_send.at[o], z_recv.at[o], {"dom": z_peer(o)})

    here = pl.ds(pl.multiple_of(xi * side + zi * piece, 8), piece)

    def g_copy(o):
        peer = {"dom": lax.rem(d + o, doms)}
        return remote(weight_out.at[here], weight_out.at[here], g_send.at[o], g_recv.at[o], peer)

    def side_rows(x, p=0, many=side):
        return pl.ds(pl.multiple_of(EXTRA + x * side + p * piece, 8), many)

    for h in range(2):
        plane = 1 - high if h == 0 else high
        cut = lambda c, many: pl.ds(pl.multiple_of((plane * 2 + c) * quarter, quarter), many)
        both = lax.dot_general(
            agg[...], dpre[:, cut(0, 2 * quarter)], (((0,), (0,)), ((), ())), preferred_element_type=f32
        )
        for c in range(2):
            part[h, c, pl.ds(EXTRA, width), :] = both[:, c * quarter : (c + 1) * quarter]
            part[h, c, pl.ds(0, EXTRA), :] = extras[:, cut(c, quarter)]
        core_copy(h).start()

    core_copy(0).wait_recv()
    edge = part[0, low, pl.ds(0, EXTRA), :] + recv_core[0, pl.ds(0, EXTRA), :]
    edge_high = edge.astype(bf16).astype(f32)
    edge_both = jnp.concatenate([edge_high, edge - edge_high], axis=0).astype(bf16)
    for k, x in ((1, 1 - xi), (0, xi)):
        send_y[k, pl.ds(0, 2 * EXTRA), :] = edge_both
        send_y[k, pl.ds(2 * EXTRA, side), :] = (
            part[0, low, side_rows(x), :] + recv_core[0, side_rows(x), :]
        ).astype(bf16)
        y_copy(k).start()
    core_copy(1).wait_recv()
    edge = part[1, low, pl.ds(0, EXTRA), :] + recv_core[1, pl.ds(0, EXTRA), :]
    send_x[pl.ds(0, EXTRA), :] = edge
    send_x[pl.ds(EXTRA, side), :] = part[1, low, side_rows(1 - xi), :] + recv_core[1, side_rows(1 - xi), :]
    x_copy().start()
    for k in range(2):
        y_copy(k).wait_recv()
    x_copy().wait_recv()
    edge += arrive_x[pl.ds(0, EXTRA), :]
    for k in range(2):
        edge_both = arrive_y[k, pl.ds(0, 2 * EXTRA), :].astype(f32)
        edge += edge_both[:EXTRA] + edge_both[EXTRA:]
    for p in range(depth):
        half[p, pl.ds(0, EXTRA), :] = edge
    for p in range(0, depth, 2):
        sums = part[1, low, side_rows(xi, p, 2 * piece), :] + recv_core[1, side_rows(xi, p, 2 * piece), :]
        sums += arrive_x[pl.ds(EXTRA + p * piece, 2 * piece), :]
        for k in range(2):
            sums += arrive_y[k, pl.ds(2 * EXTRA + p * piece, 2 * piece), :].astype(f32)
        for q in range(2):
            half[p + q, pl.ds(EXTRA, piece), :] = sums[q * piece : (q + 1) * piece]

    @pl.loop(1, depth)
    def _(o):
        z_copy(o).start()

    @pl.loop(1, depth)
    def _(o):
        z_copy(o).wait_recv()

    sums = half[zi]
    for o in range(1, depth):
        sums += recv_z[o]
    weight_out[here, :] = sums[EXTRA:]

    @pl.loop(1, doms)
    def _(o):
        g_copy(o).start()

    bias_out[...] = sums[0:1]
    gain_out[...] = sums[1:2]
    for k in range(2):
        core_copy(k).wait_send()
        y_copy(k).wait_send()
    x_copy().wait_send()

    @pl.loop(1, depth)
    def _(o):
        z_copy(o).wait_send()

    @pl.loop(1, doms)
    def _(o):
        g_copy(o).wait()


def step(cfg, requests, feat, adj, mask, token, weight, bias, gain, first, second, count, words):
    doms, own, wanted, lanes, slot_count = cfg
    nblocks, block, width = feat.shape
    quarter = weight.shape[1]
    total = own + wanted
    depth = doms // 2
    side = width // 2
    dma = pltpu.SemaphoreType.DMA
    anywhere = pl.BlockSpec(memory_space=pltpu.HBM)
    return pl.pallas_call(
        functools.partial(step_kernel, cfg),
        in_specs=[pl.BlockSpec(memory_space=pltpu.SMEM)] + [anywhere] * 11,
        out_specs=[pl.BlockSpec(memory_space=pltpu.VMEM)] * 3,
        out_shape=(
            jax.ShapeDtypeStruct((width, quarter), f32),
            jax.ShapeDtypeStruct((1, quarter), f32),
            jax.ShapeDtypeStruct((1, quarter), f32),
        ),
        scratch_shapes=[
            pltpu.VMEM(feat.shape, bf16),
            pltpu.VMEM(adj.shape, bf16),
            pltpu.VMEM(mask.shape, jnp.int32),
            pltpu.VMEM(token.shape, bf16),
            pltpu.VMEM(bias.shape, bf16),
            pltpu.VMEM(gain.shape, f32),
            pltpu.VMEM(first.shape, jnp.int32),
            pltpu.VMEM(second.shape, jnp.int32),
            pltpu.VMEM(count.shape, jnp.int32),
            pltpu.VMEM(words.shape, jnp.int32),
            pltpu.VMEM((width + 16, width), bf16),
            pltpu.VMEM((width + 16, quarter), bf16),
            pltpu.VMEM((slot_count, block, width), bf16),
            pltpu.VMEM((wanted, block, width), bf16),
            pltpu.VMEM((total * block, width), bf16),
            pltpu.VMEM((total * block, width), bf16),
            pltpu.VMEM((own * block, width), bf16),
            pltpu.VMEM((total * block, width), f32),
            pltpu.VMEM((total, own * block, block), f32),
            pltpu.VMEM((total * own, block), f32),
            pltpu.VMEM((own * block, total * block), bf16),
            pltpu.VMEM((own * block, width), f32),
            pltpu.VMEM((own * block, width), f32),
            pltpu.VMEM((total * block, width), bf16),
            pltpu.VMEM((2, 2, EXTRA + width, quarter), f32),
            pltpu.VMEM((2, EXTRA + width, quarter), f32),
            pltpu.VMEM((2, 2 * EXTRA + side, quarter), bf16),
            pltpu.VMEM((2, 2 * EXTRA + side, quarter), bf16),
            pltpu.VMEM((EXTRA + side, quarter), f32),
            pltpu.VMEM((EXTRA + side, quarter), f32),
            pltpu.VMEM((depth, EXTRA + side // depth, quarter), f32),
            pltpu.VMEM((depth, EXTRA + side // depth, quarter), f32),
            pltpu.VMEM((1, width), f32),
            pltpu.VMEM((EXTRA, width), f32),
            dma((11,)), dma((3,)), dma((3,)), dma((slot_count,)), dma((wanted,)),
            dma((2,)), dma((2,)), dma((2,)), dma((2,)), dma, dma,
            dma((depth,)), dma((depth,)), dma((doms,)), dma((doms,)),
        ],
        compiler_params=pltpu.CompilerParams(collective_id=0, has_side_effects=True, vmem_limit_bytes=LIMIT),
    )(requests, feat, adj, mask, token, weight, bias, gain, first, second, count, words)


def body(
    features, adjacency, node_mask, mask_token, enc_weight, enc_bias, gain, requests,
    pair_first, pair_second, label_words, pair_count,
):
    nodes, width = features.shape
    block = adjacency.shape[1]
    nblocks = nodes // block
    doms = lax.axis_size("dom")
    lanes = lax.axis_size("tp")
    slots = pair_first.shape[2]
    wanted = doms // lanes
    cfg = doms, nblocks // lanes, wanted, lanes, 3 if (doms, lanes) == (8, 4) else wanted
    weight_grad, bias_grad, gain_grad = step(
        cfg, requests.reshape(doms),
        features.reshape(nblocks, block, width),
        adjacency.reshape(nblocks, block, block),
        node_mask.reshape(nblocks, 1, block),
        mask_token.reshape(width // 128, 128), enc_weight, enc_bias.reshape(1, -1), gain.reshape(1, width),
        pair_first.reshape(1, slots), pair_second.reshape(1, slots), pair_count.reshape(1, 1),
        label_words.reshape(slots * label_words.shape[3], block),
    )
    return weight_grad, bias_grad.reshape(-1), gain_grad.reshape(-1)


def solution(mesh):
    placed = (
        P("dom", None),
        P("dom", None),
        P("dom"),
        P(),
        P(None, "tp"),
        P("tp"),
        P(),
        P(None, "dom"),
        P("dom", "tp", None),
        P("dom", "tp", None),
        P("dom", "tp", None, None, None),
        P("dom", "tp"),
    )
    return jax.shard_map(
        body,
        mesh=mesh,
        in_specs=placed,
        out_specs=(P(None, "tp"), P("tp"), P("tp")),
        check_vma=False,
    )
```

```python
import functools

import jax
import jax.numpy as jnp
from jax import lax
from jax.experimental import pallas as pl
from jax.experimental.pallas import tpu as pltpu
from jax.sharding import PartitionSpec as P

NORM = 256.0
WORD = 16
EXTRA = 8
MESH = pl.DeviceIdType.MESH
LIMIT = 60 * 1024 * 1024
f32 = jnp.float32
bf16 = jnp.bfloat16


def served(lane):
    return lax.rem(lane, 2) * 2 + lax.div(lane, 2)


def slope_tile(half_logits, tilt, half_live):
    return (half_live * jnp.tanh(half_logits) + tilt).astype(bf16)


def rows_of(k, block, many=1):
    start = k * block
    if not isinstance(start, int):
        start = pl.multiple_of(start, block)
    return pl.ds(start, many * block)


def step_kernel(
    cfg, requests, feat_hbm, adj_hbm, mask_hbm, token_hbm, weight_hbm, bias_hbm, gain_hbm,
    first_hbm, second_hbm, count_hbm, words_hbm,
    weight_out, bias_out, gain_out,
    feat, adj, mask, token, bias, gain, first, second, count, words,
    gathered, packed, asked, landed, agg, z, scaled, curve, tilt, live, slope, first_acc, second_acc, dpre,
    part, recv_core, leave, arrive, half, recv_z, far_bias, extras,
    feat_sem, w_send, w_recv, a_send, a_recv, core_send, core_recv, plane_send, plane_recv,
    z_send, z_recv, g_send, g_recv,
):
    doms, own, wanted, lanes, slot_count = cfg
    depth = doms // 2
    d = lax.axis_index("dom")
    t = lax.axis_index("tp")
    low = lax.rem(t, 2)
    high = lax.div(t, 2)
    core_peer = high * 2 + (1 - low)
    y_peer = (1 - high) * 2 + low
    xi = lax.rem(d, 2)
    zi = lax.div(d, 2)
    x_peer = zi * 2 + (1 - xi)
    a = lax.div(d, wanted)
    j = lax.rem(d, wanted)
    width, quarter = weight_hbm.shape
    block = mask.shape[2]

    def z_peer(o):
        return lax.rem(zi + o, depth) * 2 + xi

    pairs = (
        (weight_hbm, packed.at[pl.ds(0, width)]), (bias_hbm, bias), (token_hbm, token), (mask_hbm, mask),
        (gain_hbm, gain), (first_hbm, first), (second_hbm, second), (count_hbm, count),
    )
    for o in range(lanes):
        group = lax.rem(t + o, lanes) * own
        span = pl.ds(group, own)
        pairs += ((adj_hbm.at[span], adj.at[span]),)
        for part_of in range(0, own, own // 2):
            span = pl.ds(group + part_of, own // 2)
            pairs += ((feat_hbm.at[span], feat.at[span]),)
        if o == 0:
            early_fetches = len(pairs)
    pairs += ((words_hbm, words),)
    fetches = [pltpu.make_async_copy(source, target, feat_sem.at[k]) for k, (source, target) in enumerate(pairs)]
    for fetch in fetches:
        fetch.start()

    barrier = pltpu.get_barrier_semaphore()

    def greet(peer):
        pl.semaphore_signal(barrier, inc=1, device_id=peer, device_id_type=MESH)

    greet({"tp": core_peer})
    greet({"tp": y_peer})

    @pl.loop(1, doms)
    def _(o):
        greet({"dom": lax.rem(d + o, doms)})

    greet((x_peer, y_peer))

    if slot_count == 3:
        home = high == lax.div(zi, 2)
        near_z = 2 * lax.div(zi, 2) + low
        far_z = 2 * (1 - lax.div(zi, 2)) + low
        outgoing = (
            (None, far_z * 2 + jnp.where(home, xi, 1 - xi)),
            (home, near_z * 2 + xi),
            (home, near_z * 2 + 1 - xi),
        )
        mine_slot = 1
        alone = zi == t

        def lane_from(jj):
            same_half = lax.div(zi, 2) == high
            straight = jnp.logical_or(same_half, xi == jj)
            return jnp.where(straight, high, 1 - high) * 2 + lax.rem(zi, 2)

        sends = 1 + jnp.where(home, 2, 0)
    else:
        outgoing = tuple((None, served(t) * wanted + lax.rem(j + c, wanted)) for c in range(wanted))
        mine_slot = 0
        alone = jnp.logical_and(a == t, served(t) == t)

        def lane_from(jj):
            return served(a)

        sends = wanted

    def when_sent(c, do):
        active = outgoing[c][0]
        if c == mine_slot:
            other = jnp.logical_not(alone)
            active = other if active is None else jnp.logical_and(active, other)
        if active is None:
            do()
        else:
            pl.when(active)(do)

    def when_from(jj, do):
        pl.when(jnp.logical_not(jnp.logical_and(alone, j == jj)))(do)

    for c in range(slot_count):
        when_sent(c, functools.partial(greet, (outgoing[c][1], a)))
    for jj in range(wanted):
        when_from(jj, functools.partial(greet, (t * wanted + jj, lane_from(jj))))

    columns = lambda c: pl.ds(pl.multiple_of(c * quarter, quarter), quarter)
    fetches[0].wait()
    fetches[1].wait()
    packed[pl.ds(width, 16), :] = jnp.broadcast_to(bias[...], (16, quarter))
    gathered[:, columns(t)] = packed[...]
    pl.semaphore_wait(barrier, 2 + doms + wanted + sends - jnp.where(alone, 2, 0))

    def weight_copy(k, source, column, peer):
        return pltpu.make_async_remote_copy(
            src_ref=source, dst_ref=gathered.at[:, columns(column)],
            send_sem=w_send.at[k], recv_sem=w_recv.at[k],
            device_id={"tp": peer}, device_id_type=MESH,
        )

    across = weight_copy(0, packed, t, y_peer)
    near = weight_copy(1, packed, t, core_peer)
    relay = weight_copy(2, gathered.at[:, columns(y_peer)], y_peer, core_peer)
    across.start()
    near.start()

    rows = lax.broadcasted_iota(jnp.int32, (block, block), 0)
    cols = lax.broadcasted_iota(jnp.int32, (block, block), 1)
    for fetch in fetches[2:early_fetches]:
        fetch.wait()
    token32 = token[...].astype(f32)
    token_row = jnp.concatenate([token32[k : k + 1, :] for k in range(token32.shape[0])], axis=1)

    def aggregate(node_block):
        hidden = jnp.sum(jnp.where(rows == cols, mask[node_block].astype(f32), 0.0), axis=1, keepdims=True)
        masked32 = jnp.where(hidden == 1.0, token_row, feat[node_block].astype(f32))
        mixed = jnp.dot(adj[node_block], masked32.astype(bf16), preferred_element_type=f32)
        return (masked32 + mixed).astype(bf16)

    for k in range(own):
        agg[rows_of(k, block), :] = aggregate(t * own + k)

    for fetch in fetches[early_fetches:]:
        fetch.wait()

    def agg_copy(c, slot):
        return pltpu.make_async_remote_copy(
            src_ref=asked.at[c], dst_ref=landed.at[slot],
            send_sem=a_send.at[c], recv_sem=a_recv.at[slot],
            device_id=(outgoing[c][1], a), device_id_type=MESH,
        )

    for c in range(slot_count):
        asked[c] = aggregate(requests[outgoing[c][1]])
        when_sent(c, lambda c=c: agg_copy(c, j).start())

    @pl.when(alone)
    def _():
        landed[j] = asked[mine_slot]

    slots = first.shape[1]
    cells = own * (own + wanted)
    key = second[...] * own + first[...]
    cell = lax.broadcasted_iota(jnp.int32, (cells, slots), 0)
    slot = lax.broadcasted_iota(jnp.int32, (cells, slots), 1)
    hot32 = jnp.where(jnp.logical_and(cell == key, slot < count[...]), 1.0, 0.0)
    live[...] = jnp.broadcast_to(0.5 * jnp.sum(hot32, axis=1, keepdims=True), (cells, block))
    hot = hot32.astype(bf16)

    def count_labels(w):
        word = words[pl.ds(w, slots, stride=block // WORD), :]
        for b in range(0, WORD, 2):
            bits = jnp.concatenate(
                [jnp.where(jnp.bitwise_and(word, 1 << (b + q)) == 0, 0.5, -0.5).astype(bf16) for q in range(2)], axis=1
            )
            counts = jnp.dot(hot, bits, preferred_element_type=f32)
            for q in range(2):
                for ib in range(own + wanted):
                    tilt[ib, pl.ds(w * WORD + b + q, own, stride=block), :] = counts[
                        ib * own : (ib + 1) * own, q * block : (q + 1) * block
                    ]

    early = block // WORD // 2
    pl.loop(0, early)(count_labels)
    across.wait_recv()
    relay.start()
    pl.loop(early, block // WORD)(count_labels)
    near.wait_recv()
    relay.wait_recv()

    matrix = gathered[:width, :]
    shift = gathered[width : width + 1, :].astype(f32)
    half_gain = 0.5 * gain[...]

    def activate(k):
        spot = rows_of(k, block, 2)
        pre = jnp.dot(agg[spot, :], matrix, preferred_element_type=f32) + shift
        sig = 0.5 * jnp.tanh(0.5 * pre) + 0.5
        curve[spot, :] = sig * (1.0 + pre * (1.0 - sig)) * (2.0 / NORM)
        value = (pre * sig).astype(bf16)
        z[spot, :] = value
        return value

    for k in range(0, own, 2):
        value = activate(k)
        scaled[rows_of(k, block, 2), :] = (value.astype(f32) * half_gain).astype(bf16)

    def score(k, ib):
        logits = lax.dot_general(
            scaled[rows_of(k, block, 2), :], z[rows_of(ib, block, 2), :], (((1,), (1,)), ((), ())),
            preferred_element_type=f32,
        )
        for q in range(2):
            for r in range(2):
                slope[rows_of(k + q, block), rows_of(ib + r, block)] = slope_tile(
                    logits[q * block : (q + 1) * block, r * block : (r + 1) * block],
                    tilt[ib + r, rows_of(k + q, block), :],
                    live[pl.ds((ib + r) * own + k + q, 1), :],
                )

    mine = pl.ds(0, own * block)
    for k in range(0, own, 2):
        for ib in range(0, own, 2):
            score(k, ib)
        first_acc[rows_of(k, block, 2), :] = jnp.dot(
            slope[rows_of(k, block, 2), mine], z[mine, :], preferred_element_type=f32
        )

    def second_of(ib):
        return lax.dot_general(
            slope[:, rows_of(ib, block, 2)], scaled[...], (((0,), (0,)), ((), ())), preferred_element_type=f32
        )

    for ib in range(0, own, 2):
        second_acc[rows_of(ib, block, 2), :] = second_of(ib)

    for jj in range(wanted):
        when_from(jj, lambda jj=jj: agg_copy(0, jj).wait_recv())
    for c in range(slot_count):
        when_sent(c, lambda c=c: agg_copy(c, j).wait_send())
    across.wait_send()
    near.wait_send()
    relay.wait_send()

    far_bias[...] = jnp.zeros_like(far_bias)

    @pl.loop(0, wanted // 2)
    def _(step):
        ib = own + 2 * step
        spot = rows_of(ib, block, 2)
        agg[spot, :] = landed[pl.ds(2 * step, 2)].reshape(2 * block, width)
        value = activate(ib)
        for k in range(0, own, 2):
            score(k, ib)
            first_acc[rows_of(k, block, 2), :] += jnp.dot(
                slope[rows_of(k, block, 2), spot], value, preferred_element_type=f32
            )
        change = second_of(ib) * curve[spot, :]
        dpre[spot, :] = change.astype(bf16)
        far_bias[...] += jnp.sum(change, axis=0, keepdims=True)

    bias_sum = far_bias[...]
    gain_sum = jnp.zeros((1, width), f32)
    for k in range(0, own, 2):
        spot = rows_of(k, block, 2)
        value = first_acc[spot, :]
        gain_sum += jnp.sum(z[spot, :].astype(f32) * value, axis=0, keepdims=True)
        value = (half_gain * value + second_acc[spot, :]) * curve[spot, :]
        bias_sum += jnp.sum(value, axis=0, keepdims=True)
        dpre[spot, :] = value.astype(bf16)
    gain_sum = gain_sum * (1.0 / NORM)
    row = lax.broadcasted_iota(jnp.int32, (EXTRA, width), 0)
    extra = jnp.where(row == 0, bias_sum, jnp.where(row == 1, gain_sum, 0.0))
    extras[...] = extra

    side = width // 2
    piece = side // depth

    def remote(source, target, send, recv, peer):
        return pltpu.make_async_remote_copy(
            src_ref=source, dst_ref=target, send_sem=send, recv_sem=recv, device_id=peer, device_id_type=MESH
        )

    def core_copy(h):
        return remote(part.at[h, 1 - low], recv_core.at[h], core_send.at[h], core_recv.at[h], {"tp": core_peer})

    plane_peers = (d, y_peer), (x_peer, y_peer), (x_peer, t)

    def plane_copy(k):
        return remote(leave.at[k], arrive.at[k], plane_send.at[k], plane_recv.at[k], plane_peers[k])

    def pack_plane(k, h, x, edge):
        edge_high = edge.astype(bf16).astype(f32)
        leave[k, pl.ds(0, 2 * EXTRA), :] = jnp.concatenate([edge_high, edge - edge_high], axis=0).astype(bf16)
        leave[k, pl.ds(2 * EXTRA, side), :] = (
            part[h, low, side_rows(x), :] + recv_core[h, side_rows(x), :]
        ).astype(bf16)
        plane_copy(k).start()

    def z_copy(o):
        p = lax.rem(zi + o, depth)
        return remote(half.at[p], recv_z.at[o], z_send.at[o], z_recv.at[o], {"dom": z_peer(o)})

    here = pl.ds(pl.multiple_of(xi * side + zi * piece, 8), piece)

    def g_copy(o):
        peer = {"dom": lax.rem(d + o, doms)}
        return remote(weight_out.at[here], weight_out.at[here], g_send.at[o], g_recv.at[o], peer)

    def side_rows(x, p=0, many=side):
        return pl.ds(pl.multiple_of(EXTRA + x * side + p * piece, 8), many)

    for h in range(2):
        plane = 1 - high if h == 0 else high
        cut = lambda c, many: pl.ds(pl.multiple_of((plane * 2 + c) * quarter, quarter), many)
        both = lax.dot_general(
            agg[...], dpre[:, cut(0, 2 * quarter)], (((0,), (0,)), ((), ())), preferred_element_type=f32
        )
        for c in range(2):
            part[h, c, pl.ds(EXTRA, width), :] = both[:, c * quarter : (c + 1) * quarter]
            part[h, c, pl.ds(0, EXTRA), :] = extras[:, cut(c, quarter)]
        core_copy(h).start()

    core_copy(0).wait_recv()
    edge = part[0, low, pl.ds(0, EXTRA), :] + recv_core[0, pl.ds(0, EXTRA), :]
    pack_plane(1, 0, 1 - xi, edge)
    pack_plane(0, 0, xi, edge)
    core_copy(1).wait_recv()
    edge = part[1, low, pl.ds(0, EXTRA), :] + recv_core[1, pl.ds(0, EXTRA), :]
    pack_plane(2, 1, 1 - xi, edge)
    for k in range(3):
        plane_copy(k).wait_recv()
    for k in range(3):
        edge_both = arrive[k, pl.ds(0, 2 * EXTRA), :].astype(f32)
        edge += edge_both[:EXTRA] + edge_both[EXTRA:]
    for p in range(depth):
        half[p, pl.ds(0, EXTRA), :] = edge
    for p in range(0, depth, 2):
        sums = part[1, low, side_rows(xi, p, 2 * piece), :] + recv_core[1, side_rows(xi, p, 2 * piece), :]
        for k in range(3):
            sums += arrive[k, pl.ds(2 * EXTRA + p * piece, 2 * piece), :].astype(f32)
        for q in range(2):
            half[p + q, pl.ds(EXTRA, piece), :] = sums[q * piece : (q + 1) * piece]

    @pl.loop(1, depth)
    def _(o):
        z_copy(o).start()

    @pl.loop(1, depth)
    def _(o):
        z_copy(o).wait_recv()

    sums = half[zi]
    for o in range(1, depth):
        sums += recv_z[o]
    weight_out[here, :] = sums[EXTRA:]

    @pl.loop(1, doms)
    def _(o):
        g_copy(o).start()

    bias_out[...] = sums[0:1]
    gain_out[...] = sums[1:2]
    for k in range(2):
        core_copy(k).wait_send()
    for k in range(3):
        plane_copy(k).wait_send()

    @pl.loop(1, depth)
    def _(o):
        z_copy(o).wait_send()

    @pl.loop(1, doms)
    def _(o):
        g_copy(o).wait()


def step(cfg, requests, feat, adj, mask, token, weight, bias, gain, first, second, count, words):
    doms, own, wanted, lanes, slot_count = cfg
    nblocks, block, width = feat.shape
    quarter = weight.shape[1]
    total = own + wanted
    depth = doms // 2
    side = width // 2
    dma = pltpu.SemaphoreType.DMA
    anywhere = pl.BlockSpec(memory_space=pltpu.HBM)
    return pl.pallas_call(
        functools.partial(step_kernel, cfg),
        in_specs=[pl.BlockSpec(memory_space=pltpu.SMEM)] + [anywhere] * 11,
        out_specs=[pl.BlockSpec(memory_space=pltpu.VMEM)] * 3,
        out_shape=(
            jax.ShapeDtypeStruct((width, quarter), f32),
            jax.ShapeDtypeStruct((1, quarter), f32),
            jax.ShapeDtypeStruct((1, quarter), f32),
        ),
        scratch_shapes=[
            pltpu.VMEM(feat.shape, bf16),
            pltpu.VMEM(adj.shape, bf16),
            pltpu.VMEM(mask.shape, jnp.int32),
            pltpu.VMEM(token.shape, bf16),
            pltpu.VMEM(bias.shape, bf16),
            pltpu.VMEM(gain.shape, f32),
            pltpu.VMEM(first.shape, jnp.int32),
            pltpu.VMEM(second.shape, jnp.int32),
            pltpu.VMEM(count.shape, jnp.int32),
            pltpu.VMEM(words.shape, jnp.int32),
            pltpu.VMEM((width + 16, width), bf16),
            pltpu.VMEM((width + 16, quarter), bf16),
            pltpu.VMEM((slot_count, block, width), bf16),
            pltpu.VMEM((wanted, block, width), bf16),
            pltpu.VMEM((total * block, width), bf16),
            pltpu.VMEM((total * block, width), bf16),
            pltpu.VMEM((own * block, width), bf16),
            pltpu.VMEM((total * block, width), f32),
            pltpu.VMEM((total, own * block, block), f32),
            pltpu.VMEM((total * own, block), f32),
            pltpu.VMEM((own * block, total * block), bf16),
            pltpu.VMEM((own * block, width), f32),
            pltpu.VMEM((own * block, width), f32),
            pltpu.VMEM((total * block, width), bf16),
            pltpu.VMEM((2, 2, EXTRA + width, quarter), f32),
            pltpu.VMEM((2, EXTRA + width, quarter), f32),
            pltpu.VMEM((3, 2 * EXTRA + side, quarter), bf16),
            pltpu.VMEM((3, 2 * EXTRA + side, quarter), bf16),
            pltpu.VMEM((depth, EXTRA + side // depth, quarter), f32),
            pltpu.VMEM((depth, EXTRA + side // depth, quarter), f32),
            pltpu.VMEM((1, width), f32),
            pltpu.VMEM((EXTRA, width), f32),
            dma((9 + 3 * lanes,)), dma((3,)), dma((3,)), dma((slot_count,)), dma((wanted,)),
            dma((2,)), dma((2,)), dma((3,)), dma((3,)),
            dma((depth,)), dma((depth,)), dma((doms,)), dma((doms,)),
        ],
        compiler_params=pltpu.CompilerParams(collective_id=0, has_side_effects=True, vmem_limit_bytes=LIMIT),
    )(requests, feat, adj, mask, token, weight, bias, gain, first, second, count, words)


def body(
    features, adjacency, node_mask, mask_token, enc_weight, enc_bias, gain, requests,
    pair_first, pair_second, label_words, pair_count,
):
    nodes, width = features.shape
    block = adjacency.shape[1]
    nblocks = nodes // block
    doms = lax.axis_size("dom")
    lanes = lax.axis_size("tp")
    slots = pair_first.shape[2]
    wanted = doms // lanes
    cfg = doms, nblocks // lanes, wanted, lanes, 3 if (doms, lanes) == (8, 4) else wanted
    weight_grad, bias_grad, gain_grad = step(
        cfg, requests.reshape(doms),
        features.reshape(nblocks, block, width),
        adjacency.reshape(nblocks, block, block),
        node_mask.reshape(nblocks, 1, block),
        mask_token.reshape(width // 128, 128), enc_weight, enc_bias.reshape(1, -1), gain.reshape(1, width),
        pair_first.reshape(1, slots), pair_second.reshape(1, slots), pair_count.reshape(1, 1),
        label_words.reshape(slots * label_words.shape[3], block),
    )
    return weight_grad, bias_grad.reshape(-1), gain_grad.reshape(-1)


def solution(mesh):
    placed = (
        P("dom", None),
        P("dom", None),
        P("dom"),
        P(),
        P(None, "tp"),
        P("tp"),
        P(),
        P(None, "dom"),
        P("dom", "tp", None),
        P("dom", "tp", None),
        P("dom", "tp", None, None, None),
        P("dom", "tp"),
    )
    return jax.shard_map(
        body,
        mesh=mesh,
        in_specs=placed,
        out_specs=(P(None, "tp"), P("tp"), P("tp")),
        check_vma=False,
    )
```

```python
import functools

import jax
import jax.numpy as jnp
from jax import lax
from jax.experimental import pallas as pl
from jax.experimental.pallas import tpu as pltpu
from jax.sharding import PartitionSpec as P

NORM = 256.0
WORD = 16
PACK = 256.0
EXTRA = 8
PIECES = 2
MESH = pl.DeviceIdType.MESH
LIMIT = 60 * 1024 * 1024
f32 = jnp.float32
bf16 = jnp.bfloat16


def served(lane):
    return lax.rem(lane, 2) * 2 + lax.div(lane, 2)


def slope_tile(half_logits, packed_counts, half_live):
    upper = jnp.floor(packed_counts * (1.0 / PACK))
    lower = packed_counts - PACK * upper
    counts = jnp.concatenate(
        [half[k : k + 8] for k in range(0, packed_counts.shape[0], 8) for half in (lower, upper)], axis=0
    )
    return (half_live * jnp.tanh(half_logits) + (half_live - counts)).astype(bf16)


def rows_of(k, block, many=1):
    start = k * block
    if not isinstance(start, int):
        start = pl.multiple_of(start, block)
    return pl.ds(start, many * block)


def step_kernel(
    cfg, requests, feat_hbm, adj_hbm, mask_hbm, token_hbm, weight_hbm, bias_hbm, gain_hbm,
    first_hbm, second_hbm, count_hbm, words_hbm,
    result,
    feat, adj, mask, token, bias, gain, first, second, count, words,
    gathered, packed, asked, landed, agg, z, turned, scaled, curve, marks, live, slope, first_acc, second_acc, dpre,
    part, recv_core, leave, arrive, half, recv_z, far_bias, extras,
    feat_sem, w_send, w_recv, a_send, a_recv, core_send, core_recv, plane_send, plane_recv,
    z_send, z_recv, g_send, g_recv,
):
    doms, own, wanted, lanes, slot_count = cfg
    depth = doms // 2
    d = lax.axis_index("dom")
    t = lax.axis_index("tp")
    low = lax.rem(t, 2)
    high = lax.div(t, 2)
    core_peer = high * 2 + (1 - low)
    y_peer = (1 - high) * 2 + low
    xi = lax.rem(d, 2)
    zi = lax.div(d, 2)
    x_peer = zi * 2 + (1 - xi)
    a = lax.div(d, wanted)
    j = lax.rem(d, wanted)
    width, quarter = weight_hbm.shape
    block = mask.shape[2]

    def z_peer(o):
        return lax.rem(zi + o, depth) * 2 + xi

    pairs = (
        (weight_hbm, packed.at[pl.ds(0, width)]), (bias_hbm, bias), (token_hbm, token), (mask_hbm, mask),
        (gain_hbm, gain), (first_hbm, first), (second_hbm, second), (count_hbm, count),
    )
    for o in range(lanes):
        group = lax.rem(t + o, lanes) * own
        span = pl.ds(group, own)
        pairs += ((adj_hbm.at[span], adj.at[span]),)
        for part_of in range(0, own, own // 2):
            span = pl.ds(group + part_of, own // 2)
            pairs += ((feat_hbm.at[span], feat.at[span]),)
        if o == 0:
            early_fetches = len(pairs)
    pairs += ((words_hbm, words),)
    fetches = [pltpu.make_async_copy(source, target, feat_sem.at[k]) for k, (source, target) in enumerate(pairs)]
    for fetch in fetches:
        fetch.start()

    barrier = pltpu.get_barrier_semaphore()

    def greet(peer):
        pl.semaphore_signal(barrier, inc=1, device_id=peer, device_id_type=MESH)

    greet({"tp": core_peer})
    greet({"tp": y_peer})

    @pl.loop(1, doms)
    def _(o):
        greet({"dom": lax.rem(d + o, doms)})

    greet((x_peer, y_peer))

    if slot_count == 3:
        home = high == lax.div(zi, 2)
        near_z = 2 * lax.div(zi, 2) + low
        far_z = 2 * (1 - lax.div(zi, 2)) + low
        outgoing = (
            (None, far_z * 2 + jnp.where(home, xi, 1 - xi)),
            (home, near_z * 2 + xi),
            (home, near_z * 2 + 1 - xi),
        )
        mine_slot = 1
        alone = zi == t

        def lane_from(jj):
            same_half = lax.div(zi, 2) == high
            straight = jnp.logical_or(same_half, xi == jj)
            return jnp.where(straight, high, 1 - high) * 2 + lax.rem(zi, 2)

        sends = 1 + jnp.where(home, 2, 0)
    else:
        outgoing = tuple((None, served(t) * wanted + lax.rem(j + c, wanted)) for c in range(wanted))
        mine_slot = 0
        alone = jnp.logical_and(a == t, served(t) == t)

        def lane_from(jj):
            return served(a)

        sends = wanted

    def when_sent(c, do):
        active = outgoing[c][0]
        if c == mine_slot:
            other = jnp.logical_not(alone)
            active = other if active is None else jnp.logical_and(active, other)
        if active is None:
            do()
        else:
            pl.when(active)(do)

    def when_from(jj, do):
        pl.when(jnp.logical_not(jnp.logical_and(alone, j == jj)))(do)

    for c in range(slot_count):
        when_sent(c, functools.partial(greet, (outgoing[c][1], a)))
    for jj in range(wanted):
        when_from(jj, functools.partial(greet, (t * wanted + jj, lane_from(jj))))

    columns = lambda c: pl.ds(pl.multiple_of(c * quarter, quarter), quarter)
    fetches[0].wait()
    fetches[1].wait()
    packed[pl.ds(width, 16), :] = jnp.broadcast_to(bias[...], (16, quarter))
    gathered[:, columns(t)] = packed[...]
    pl.semaphore_wait(barrier, 2 + doms + wanted + sends - jnp.where(alone, 2, 0))

    def weight_copy(k, source, column, peer):
        return pltpu.make_async_remote_copy(
            src_ref=source, dst_ref=gathered.at[:, columns(column)],
            send_sem=w_send.at[k], recv_sem=w_recv.at[k],
            device_id={"tp": peer}, device_id_type=MESH,
        )

    across = weight_copy(0, packed, t, y_peer)
    near = weight_copy(1, packed, t, core_peer)
    relay = weight_copy(2, gathered.at[:, columns(y_peer)], y_peer, core_peer)
    across.start()
    near.start()

    rows = lax.broadcasted_iota(jnp.int32, (block, block), 0)
    cols = lax.broadcasted_iota(jnp.int32, (block, block), 1)
    for fetch in fetches[2:early_fetches]:
        fetch.wait()
    token32 = token[...].astype(f32)
    token_row = jnp.concatenate([token32[k : k + 1, :] for k in range(token32.shape[0])], axis=1)

    def aggregate(node_block):
        hidden = jnp.sum(jnp.where(rows == cols, mask[node_block].astype(f32), 0.0), axis=1, keepdims=True)
        masked32 = jnp.where(hidden == 1.0, token_row, feat[node_block].astype(f32))
        mixed = jnp.dot(adj[node_block], masked32.astype(bf16), preferred_element_type=f32)
        return (masked32 + mixed).astype(bf16)

    for k in range(own):
        agg[rows_of(k, block), :] = aggregate(t * own + k)

    for fetch in fetches[early_fetches:]:
        fetch.wait()

    def agg_copy(c, slot):
        return pltpu.make_async_remote_copy(
            src_ref=asked.at[c], dst_ref=landed.at[slot],
            send_sem=a_send.at[c], recv_sem=a_recv.at[slot],
            device_id=(outgoing[c][1], a), device_id_type=MESH,
        )

    for c in range(slot_count):
        asked[c] = aggregate(requests[outgoing[c][1]])
        when_sent(c, lambda c=c: agg_copy(c, j).start())

    @pl.when(alone)
    def _():
        landed[j] = asked[mine_slot]

    slots = first.shape[1]
    cells = own * (own + wanted)
    key = second[...] * own + first[...]
    cell = lax.broadcasted_iota(jnp.int32, (cells, slots), 0)
    slot = lax.broadcasted_iota(jnp.int32, (cells, slots), 1)
    hot32 = jnp.where(jnp.logical_and(cell == key, slot < count[...]), 1.0, 0.0)
    live[...] = jnp.broadcast_to(0.5 * jnp.sum(hot32, axis=1, keepdims=True), (cells, block))
    hot = jnp.concatenate([hot32, PACK * hot32], axis=1).astype(bf16)

    def count_labels(w):
        word = words[pl.ds(w, slots, stride=block // WORD), :]

        def bit(b):
            return jnp.where(jnp.bitwise_and(word, 1 << b) == 0, 0.0, 1.0).astype(bf16)

        for b in range(0, WORD // 2, 2):
            bits = jnp.concatenate(
                [jnp.concatenate([bit(b + q), bit(b + q + WORD // 2)], axis=0) for q in range(2)], axis=1
            )
            counts = jnp.dot(hot, bits, preferred_element_type=f32)
            for q in range(2):
                for ib in range(own + wanted):
                    marks[ib, pl.ds(w * (WORD // 2) + b + q, own, stride=block // 2), :] = counts[
                        ib * own : (ib + 1) * own, q * block : (q + 1) * block
                    ]

    early = block // WORD // 2
    pl.loop(0, early)(count_labels)
    across.wait_recv()
    relay.start()
    pl.loop(early, block // WORD)(count_labels)
    near.wait_recv()
    relay.wait_recv()

    matrix = gathered[:width, :]
    shift = gathered[width : width + 1, :].astype(f32)
    half_gain = 0.5 * gain[...]

    def activate(k):
        spot = rows_of(k, block, 2)
        pre = jnp.dot(agg[spot, :], matrix, preferred_element_type=f32) + shift
        sig = 0.5 * jnp.tanh(0.5 * pre) + 0.5
        curve[spot, :] = sig * (1.0 + pre * (1.0 - sig)) * (2.0 / NORM)
        value = (pre * sig).astype(bf16)
        z[spot, :] = value
        turned[:, spot] = value.T
        return value

    for k in range(0, own, 2):
        value = activate(k)
        scaled[rows_of(k, block, 2), :] = (value.astype(f32) * half_gain).astype(bf16)

    def score(k, ib):
        logits = lax.dot_general(
            scaled[rows_of(k, block, 2), :], turned[:, rows_of(ib, block, 2)], (((1,), (0,)), ((), ())),
            preferred_element_type=f32,
        )
        for q in range(2):
            for r in range(2):
                slope[rows_of(k + q, block), rows_of(ib + r, block)] = slope_tile(
                    logits[q * block : (q + 1) * block, r * block : (r + 1) * block],
                    marks[ib + r, rows_of(k + q, block // 2), :],
                    live[pl.ds((ib + r) * own + k + q, 1), :],
                )

    mine = pl.ds(0, own * block)
    for k in range(0, own, 2):
        for ib in range(0, own, 2):
            score(k, ib)
        first_acc[rows_of(k, block, 2), :] = jnp.dot(
            slope[rows_of(k, block, 2), mine], z[mine, :], preferred_element_type=f32
        )

    def second_of(ib):
        return lax.dot_general(
            slope[:, rows_of(ib, block, 2)], scaled[...], (((0,), (0,)), ((), ())), preferred_element_type=f32
        )

    for ib in range(0, own, 2):
        second_acc[rows_of(ib, block, 2), :] = second_of(ib)

    for jj in range(wanted):
        when_from(jj, lambda jj=jj: agg_copy(0, jj).wait_recv())
    for c in range(slot_count):
        when_sent(c, lambda c=c: agg_copy(c, j).wait_send())
    across.wait_send()
    near.wait_send()
    relay.wait_send()

    far_bias[...] = jnp.zeros_like(far_bias)

    @pl.loop(0, wanted // 2)
    def _(step):
        ib = own + 2 * step
        spot = rows_of(ib, block, 2)
        agg[spot, :] = landed[pl.ds(2 * step, 2)].reshape(2 * block, width)
        value = activate(ib)
        for k in range(0, own, 2):
            score(k, ib)
            first_acc[rows_of(k, block, 2), :] += jnp.dot(
                slope[rows_of(k, block, 2), spot], value, preferred_element_type=f32
            )
        change = second_of(ib) * curve[spot, :]
        dpre[spot, :] = change.astype(bf16)
        far_bias[...] += jnp.sum(change, axis=0, keepdims=True)

    bias_sum = far_bias[...]
    gain_sum = jnp.zeros((1, width), f32)
    for k in range(0, own, 2):
        spot = rows_of(k, block, 2)
        value = first_acc[spot, :]
        gain_sum += jnp.sum(z[spot, :].astype(f32) * value, axis=0, keepdims=True)
        value = (half_gain * value + second_acc[spot, :]) * curve[spot, :]
        bias_sum += jnp.sum(value, axis=0, keepdims=True)
        dpre[spot, :] = value.astype(bf16)
    gain_sum = gain_sum * (1.0 / NORM)
    row = lax.broadcasted_iota(jnp.int32, (EXTRA, width), 0)
    extra = jnp.where(row == 0, bias_sum, jnp.where(row == 1, gain_sum, 0.0))
    extras[...] = extra

    side = width // 2
    piece = side // depth

    def remote(source, target, send, recv, peer):
        return pltpu.make_async_remote_copy(
            src_ref=source, dst_ref=target, send_sem=send, recv_sem=recv, device_id=peer, device_id_type=MESH
        )

    def core_copy(h):
        return remote(part.at[h, 1 - low], recv_core.at[h], core_send.at[h], core_recv.at[h], {"tp": core_peer})

    plane_peers = (d, y_peer), (x_peer, y_peer), (x_peer, t)

    def plane_copy(k):
        return remote(leave.at[k], arrive.at[k], plane_send.at[k], plane_recv.at[k], plane_peers[k])

    def pack_plane(k, h, x, edge):
        edge_high = edge.astype(bf16).astype(f32)
        leave[k, pl.ds(0, 2 * EXTRA), :] = jnp.concatenate([edge_high, edge - edge_high], axis=0).astype(bf16)
        leave[k, pl.ds(2 * EXTRA, side), :] = (
            part[h, low, side_rows(x), :] + recv_core[h, side_rows(x), :]
        ).astype(bf16)
        plane_copy(k).start()

    def z_copy(o):
        p = lax.rem(zi + o, depth)
        return remote(half.at[p], recv_z.at[o], z_send.at[o], z_recv.at[o], {"dom": z_peer(o)})

    here = pl.ds(pl.multiple_of(EXTRA + xi * side + zi * piece, 8), piece)

    def g_copy(o):
        peer = {"dom": lax.rem(d + o, doms)}
        return remote(result.at[here], result.at[here], g_send.at[o], g_recv.at[o], peer)

    def side_rows(x, p=0, many=side):
        return pl.ds(pl.multiple_of(EXTRA + x * side + p * piece, 8), many)

    for h in range(2):
        plane = 1 - high if h == 0 else high
        cut = lambda c, many: pl.ds(pl.multiple_of((plane * 2 + c) * quarter, quarter), many)
        both = lax.dot_general(
            agg[...], dpre[:, cut(0, 2 * quarter)], (((0,), (0,)), ((), ())), preferred_element_type=f32
        )
        for c in range(2):
            part[h, c, pl.ds(EXTRA, width), :] = both[:, c * quarter : (c + 1) * quarter]
            part[h, c, pl.ds(0, EXTRA), :] = extras[:, cut(c, quarter)]
        core_copy(h).start()

    core_copy(0).wait_recv()
    edge = part[0, low, pl.ds(0, EXTRA), :] + recv_core[0, pl.ds(0, EXTRA), :]
    pack_plane(1, 0, 1 - xi, edge)
    pack_plane(0, 0, xi, edge)
    core_copy(1).wait_recv()
    edge = part[1, low, pl.ds(0, EXTRA), :] + recv_core[1, pl.ds(0, EXTRA), :]
    pack_plane(2, 1, 1 - xi, edge)
    for k in range(3):
        plane_copy(k).wait_recv()
    for k in range(3):
        edge_both = arrive[k, pl.ds(0, 2 * EXTRA), :].astype(f32)
        edge += edge_both[:EXTRA] + edge_both[EXTRA:]
    for p in range(depth):
        half[p, pl.ds(0, EXTRA), :] = edge
    for p in range(0, depth, 2):
        sums = part[1, low, side_rows(xi, p, 2 * piece), :] + recv_core[1, side_rows(xi, p, 2 * piece), :]
        for k in range(3):
            sums += arrive[k, pl.ds(2 * EXTRA + p * piece, 2 * piece), :].astype(f32)
        for q in range(2):
            half[p + q, pl.ds(EXTRA, piece), :] = sums[q * piece : (q + 1) * piece]

    @pl.loop(1, depth)
    def _(o):
        z_copy(o).start()

    @pl.loop(1, depth)
    def _(o):
        z_copy(o).wait_recv()

    sums = half[zi]
    for o in range(1, depth):
        sums += recv_z[o]
    result[here, :] = sums[EXTRA:]

    @pl.loop(1, doms)
    def _(o):
        g_copy(o).start()

    result[pl.ds(0, EXTRA), :] = sums[:EXTRA]
    for k in range(2):
        core_copy(k).wait_send()
    for k in range(3):
        plane_copy(k).wait_send()

    @pl.loop(1, depth)
    def _(o):
        z_copy(o).wait_send()

    @pl.loop(1, doms)
    def _(o):
        g_copy(o).wait()


def step(cfg, requests, feat, adj, mask, token, weight, bias, gain, first, second, count, words):
    doms, own, wanted, lanes, slot_count = cfg
    nblocks, block, width = feat.shape
    quarter = weight.shape[1]
    total = own + wanted
    depth = doms // 2
    side = width // 2
    dma = pltpu.SemaphoreType.DMA
    anywhere = pl.BlockSpec(memory_space=pltpu.HBM)
    return pl.pallas_call(
        functools.partial(step_kernel, cfg),
        in_specs=[pl.BlockSpec(memory_space=pltpu.SMEM)] + [anywhere] * 11,
        out_specs=pl.BlockSpec(memory_space=pltpu.VMEM),
        out_shape=jax.ShapeDtypeStruct((EXTRA + width, quarter), f32),
        scratch_shapes=[
            pltpu.VMEM(feat.shape, bf16),
            pltpu.VMEM(adj.shape, bf16),
            pltpu.VMEM(mask.shape, jnp.int32),
            pltpu.VMEM(token.shape, bf16),
            pltpu.VMEM(bias.shape, bf16),
            pltpu.VMEM(gain.shape, f32),
            pltpu.VMEM(first.shape, jnp.int32),
            pltpu.VMEM(second.shape, jnp.int32),
            pltpu.VMEM(count.shape, jnp.int32),
            pltpu.VMEM(words.shape, jnp.int32),
            pltpu.VMEM((width + 16, width), bf16),
            pltpu.VMEM((width + 16, quarter), bf16),
            pltpu.VMEM((slot_count, block, width), bf16),
            pltpu.VMEM((wanted, block, width), bf16),
            pltpu.VMEM((total * block, width), bf16),
            pltpu.VMEM((total * block, width), bf16),
            pltpu.VMEM((width, total * block), bf16),
            pltpu.VMEM((own * block, width), bf16),
            pltpu.VMEM((total * block, width), f32),
            pltpu.VMEM((total, own * block // 2, block), f32),
            pltpu.VMEM((total * own, block), f32),
            pltpu.VMEM((own * block, total * block), bf16),
            pltpu.VMEM((own * block, width), f32),
            pltpu.VMEM((own * block, width), f32),
            pltpu.VMEM((total * block, width), bf16),
            pltpu.VMEM((2, 2, EXTRA + width, quarter), f32),
            pltpu.VMEM((2, EXTRA + width, quarter), f32),
            pltpu.VMEM((3, 2 * EXTRA + side, quarter), bf16),
            pltpu.VMEM((3, 2 * EXTRA + side, quarter), bf16),
            pltpu.VMEM((depth, EXTRA + side // depth, quarter), f32),
            pltpu.VMEM((depth, EXTRA + side // depth, quarter), f32),
            pltpu.VMEM((1, width), f32),
            pltpu.VMEM((EXTRA, width), f32),
            dma((9 + 3 * lanes,)), dma((3,)), dma((3,)), dma((slot_count,)), dma((wanted,)),
            dma((2,)), dma((2,)), dma((3,)), dma((3,)),
            dma((depth,)), dma((depth,)), dma((doms,)), dma((doms,)),
        ],
        compiler_params=pltpu.CompilerParams(collective_id=0, has_side_effects=True, vmem_limit_bytes=LIMIT),
    )(requests, feat, adj, mask, token, weight, bias, gain, first, second, count, words)


def emit_kernel(result, weight_out, bias_out, gain_out, held, rows_in, rows_out, sem):
    extra = pltpu.make_async_copy(result.at[pl.ds(0, EXTRA)], held.at[pl.ds(0, EXTRA)], sem)
    many = weight_out.shape[0] // PIECES
    spans = [pl.ds(k * many, many) for k in range(PIECES)]
    shifted = [pl.ds(EXTRA + k * many, many) for k in range(PIECES)]
    ins = [pltpu.make_async_copy(result.at[s], held.at[s], rows_in.at[k]) for k, s in enumerate(shifted)]
    outs = [
        pltpu.make_async_copy(held.at[s], weight_out.at[spans[k]], rows_out.at[k]) for k, s in enumerate(shifted)
    ]
    extra.start()
    for copy in ins:
        copy.start()
    extra.wait()
    bias_out[...] = held[0:1, :]
    gain_out[...] = held[1:2, :]
    for k in range(PIECES):
        ins[k].wait()
        outs[k].start()
    for copy in outs:
        copy.wait()


def emit(result):
    tall, quarter = result.shape
    vmem = pl.BlockSpec(memory_space=pltpu.VMEM)
    hbm = pl.BlockSpec(memory_space=pltpu.HBM)
    dma = pltpu.SemaphoreType.DMA
    row = jax.ShapeDtypeStruct((1, quarter), f32)
    return pl.pallas_call(
        emit_kernel,
        in_specs=[hbm],
        out_specs=[hbm, vmem, vmem],
        out_shape=(jax.ShapeDtypeStruct((tall - EXTRA, quarter), f32), row, row),
        scratch_shapes=[pltpu.VMEM((tall, quarter), f32), dma((PIECES,)), dma((PIECES,)), dma],
        compiler_params=pltpu.CompilerParams(vmem_limit_bytes=LIMIT),
    )(result)


def body(
    features, adjacency, node_mask, mask_token, enc_weight, enc_bias, gain, requests,
    pair_first, pair_second, label_words, pair_count,
):
    nodes, width = features.shape
    block = adjacency.shape[1]
    nblocks = nodes // block
    doms = lax.axis_size("dom")
    lanes = lax.axis_size("tp")
    slots = pair_first.shape[2]
    wanted = doms // lanes
    cfg = doms, nblocks // lanes, wanted, lanes, 3 if (doms, lanes) == (8, 4) else wanted
    result = step(
        cfg, requests.reshape(doms),
        features.reshape(nblocks, block, width),
        adjacency.reshape(nblocks, block, block),
        node_mask.reshape(nblocks, 1, block),
        mask_token.reshape(width // 128, 128), enc_weight, enc_bias.reshape(1, -1), gain.reshape(1, width),
        pair_first.reshape(1, slots), pair_second.reshape(1, slots), pair_count.reshape(1, 1),
        label_words.reshape(slots * label_words.shape[3], block),
    )
    weight_grad, bias_grad, gain_grad = emit(result)
    return weight_grad, bias_grad.reshape(-1), gain_grad.reshape(-1)


def solution(mesh):
    placed = (
        P("dom", None),
        P("dom", None),
        P("dom"),
        P(),
        P(None, "tp"),
        P("tp"),
        P(),
        P(None, "dom"),
        P("dom", "tp", None),
        P("dom", "tp", None),
        P("dom", "tp", None, None, None),
        P("dom", "tp"),
    )
    return jax.shard_map(
        body,
        mesh=mesh,
        in_specs=placed,
        out_specs=(P(None, "tp"), P("tp"), P("tp")),
        check_vma=False,
    )
```

```python
import functools

import jax
import jax.numpy as jnp
from jax import lax
from jax.experimental import pallas as pl
from jax.experimental.pallas import tpu as pltpu
from jax.sharding import PartitionSpec as P

NORM = 256.0
WORD = 16
PACK = 256.0
EXTRA = 8
MESH = pl.DeviceIdType.MESH
LIMIT = 60 * 1024 * 1024
f32 = jnp.float32
bf16 = jnp.bfloat16


def served(lane):
    return lax.rem(lane, 2) * 2 + lax.div(lane, 2)


def slope_tile(half_logits, packed_counts, half_live):
    upper = jnp.floor(packed_counts * (1.0 / PACK))
    lower = packed_counts - PACK * upper
    counts = jnp.concatenate(
        [half[k : k + 8] for k in range(0, packed_counts.shape[0], 8) for half in (lower, upper)], axis=0
    )
    return (half_live * jnp.tanh(half_logits) + (half_live - counts)).astype(bf16)


def rows_of(k, block, many=1):
    start = k * block
    if not isinstance(start, int):
        start = pl.multiple_of(start, block)
    return pl.ds(start, many * block)


def step_kernel(
    cfg, requests, feat_hbm, adj_hbm, mask_hbm, token_hbm, weight_hbm, bias_hbm, gain_hbm,
    first_hbm, second_hbm, count_hbm, words_hbm,
    result,
    feat, adj, mask, token, bias, gain, first, second, count, words,
    gathered, packed, asked, landed, agg, agg_turned, z, turned, scaled, curve, marks, live, slope, first_acc, second_acc, dpre,
    part, recv_core, leave, arrive, half, recv_z, far_bias, extras,
    feat_sem, w_send, w_recv, a_send, a_recv, core_send, core_recv, plane_send, plane_recv,
    z_send, z_recv, g_send, g_recv,
):
    doms, own, wanted, lanes, slot_count = cfg
    depth = doms // 2
    d = lax.axis_index("dom")
    t = lax.axis_index("tp")
    low = lax.rem(t, 2)
    high = lax.div(t, 2)
    core_peer = high * 2 + (1 - low)
    y_peer = (1 - high) * 2 + low
    xi = lax.rem(d, 2)
    zi = lax.div(d, 2)
    x_peer = zi * 2 + (1 - xi)
    a = lax.div(d, wanted)
    j = lax.rem(d, wanted)
    width, quarter = weight_hbm.shape
    block = mask.shape[2]

    def z_peer(o):
        return lax.rem(zi + o, depth) * 2 + xi

    pairs = (
        (weight_hbm, packed.at[pl.ds(0, width)]), (bias_hbm, bias), (token_hbm, token), (mask_hbm, mask),
        (gain_hbm, gain), (first_hbm, first), (second_hbm, second), (count_hbm, count),
    )
    for o in range(lanes):
        group = lax.rem(t + o, lanes) * own
        span = pl.ds(group, own)
        pairs += ((adj_hbm.at[span], adj.at[span]),)
        for part_of in range(0, own, own // 2):
            span = pl.ds(group + part_of, own // 2)
            pairs += ((feat_hbm.at[span], feat.at[span]),)
        if o == 0:
            early_fetches = len(pairs)
    pairs += ((words_hbm, words),)
    fetches = [pltpu.make_async_copy(source, target, feat_sem.at[k]) for k, (source, target) in enumerate(pairs)]
    for fetch in fetches:
        fetch.start()

    barrier = pltpu.get_barrier_semaphore()

    def greet(peer):
        pl.semaphore_signal(barrier, inc=1, device_id=peer, device_id_type=MESH)

    greet({"tp": core_peer})
    greet({"tp": y_peer})

    @pl.loop(1, doms)
    def _(o):
        greet({"dom": lax.rem(d + o, doms)})

    greet((x_peer, y_peer))

    if slot_count == 3:
        home = high == lax.div(zi, 2)
        near_z = 2 * lax.div(zi, 2) + low
        far_z = 2 * (1 - lax.div(zi, 2)) + low
        outgoing = (
            (None, far_z * 2 + jnp.where(home, xi, 1 - xi)),
            (home, near_z * 2 + xi),
            (home, near_z * 2 + 1 - xi),
        )
        mine_slot = 1
        alone = zi == t

        def lane_from(jj):
            same_half = lax.div(zi, 2) == high
            straight = jnp.logical_or(same_half, xi == jj)
            return jnp.where(straight, high, 1 - high) * 2 + lax.rem(zi, 2)

        sends = 1 + jnp.where(home, 2, 0)
    else:
        outgoing = tuple((None, served(t) * wanted + lax.rem(j + c, wanted)) for c in range(wanted))
        mine_slot = 0
        alone = jnp.logical_and(a == t, served(t) == t)

        def lane_from(jj):
            return served(a)

        sends = wanted

    def when_sent(c, do):
        active = outgoing[c][0]
        if c == mine_slot:
            other = jnp.logical_not(alone)
            active = other if active is None else jnp.logical_and(active, other)
        if active is None:
            do()
        else:
            pl.when(active)(do)

    def when_from(jj, do):
        pl.when(jnp.logical_not(jnp.logical_and(alone, j == jj)))(do)

    for c in range(slot_count):
        when_sent(c, functools.partial(greet, (outgoing[c][1], a)))
    for jj in range(wanted):
        when_from(jj, functools.partial(greet, (t * wanted + jj, lane_from(jj))))

    columns = lambda c: pl.ds(pl.multiple_of(c * quarter, quarter), quarter)
    fetches[0].wait()
    fetches[1].wait()
    packed[pl.ds(width, 16), :] = jnp.broadcast_to(bias[...], (16, quarter))
    gathered[:, columns(t)] = packed[...]
    pl.semaphore_wait(barrier, 2 + doms + wanted + sends - jnp.where(alone, 2, 0))

    def weight_copy(k, source, column, peer):
        return pltpu.make_async_remote_copy(
            src_ref=source, dst_ref=gathered.at[:, columns(column)],
            send_sem=w_send.at[k], recv_sem=w_recv.at[k],
            device_id={"tp": peer}, device_id_type=MESH,
        )

    across = weight_copy(0, packed, t, y_peer)
    near = weight_copy(1, packed, t, core_peer)
    relay = weight_copy(2, gathered.at[:, columns(y_peer)], y_peer, core_peer)
    across.start()
    near.start()

    rows = lax.broadcasted_iota(jnp.int32, (block, block), 0)
    cols = lax.broadcasted_iota(jnp.int32, (block, block), 1)
    for fetch in fetches[2:early_fetches]:
        fetch.wait()
    token32 = token[...].astype(f32)
    token_row = jnp.concatenate([token32[k : k + 1, :] for k in range(token32.shape[0])], axis=1)

    def aggregate(node_block):
        hidden = jnp.sum(jnp.where(rows == cols, mask[node_block].astype(f32), 0.0), axis=1, keepdims=True)
        masked32 = jnp.where(hidden == 1.0, token_row, feat[node_block].astype(f32))
        mixed = jnp.dot(adj[node_block], masked32.astype(bf16), preferred_element_type=f32)
        return (masked32 + mixed).astype(bf16)

    for k in range(own):
        value = aggregate(t * own + k)
        agg[rows_of(k, block), :] = value
        agg_turned[:, rows_of(k, block)] = value.T

    for fetch in fetches[early_fetches:]:
        fetch.wait()

    def agg_copy(c, slot):
        return pltpu.make_async_remote_copy(
            src_ref=asked.at[c], dst_ref=landed.at[slot],
            send_sem=a_send.at[c], recv_sem=a_recv.at[slot],
            device_id=(outgoing[c][1], a), device_id_type=MESH,
        )

    for c in range(slot_count):
        asked[c] = aggregate(requests[outgoing[c][1]])
        if slot_count == 3 and c == 0:
            pl.when(home)(lambda: agg_copy(0, j).start())
        else:
            when_sent(c, lambda c=c: agg_copy(c, j).start())

    @pl.when(alone)
    def _():
        landed[j] = asked[mine_slot]

    slots = first.shape[1]
    cells = own * (own + wanted)
    key = second[...] * own + first[...]
    cell = lax.broadcasted_iota(jnp.int32, (cells, slots), 0)
    slot = lax.broadcasted_iota(jnp.int32, (cells, slots), 1)
    hot32 = jnp.where(jnp.logical_and(cell == key, slot < count[...]), 1.0, 0.0)
    live[...] = jnp.broadcast_to(0.5 * jnp.sum(hot32, axis=1, keepdims=True), (cells, block))
    hot = jnp.concatenate([hot32, PACK * hot32], axis=1).astype(bf16)

    def count_labels(w):
        word = words[pl.ds(w, slots, stride=block // WORD), :]

        def bit(b):
            return jnp.where(jnp.bitwise_and(word, 1 << b) == 0, 0.0, 1.0).astype(bf16)

        for b in range(0, WORD // 2, 2):
            bits = jnp.concatenate(
                [jnp.concatenate([bit(b + q), bit(b + q + WORD // 2)], axis=0) for q in range(2)], axis=1
            )
            counts = jnp.dot(hot, bits, preferred_element_type=f32)
            for q in range(2):
                for ib in range(own + wanted):
                    marks[ib, pl.ds(w * (WORD // 2) + b + q, own, stride=block // 2), :] = counts[
                        ib * own : (ib + 1) * own, q * block : (q + 1) * block
                    ]

    early = block // WORD // 2
    pl.loop(0, early)(count_labels)
    across.wait_recv()
    relay.start()
    if slot_count == 3:
        pl.when(jnp.logical_not(home))(lambda: agg_copy(0, j).start())
    pl.loop(early, block // WORD)(count_labels)
    near.wait_recv()
    relay.wait_recv()

    matrix = gathered[:width, :]
    shift = gathered[width : width + 1, :].astype(f32)
    half_gain = 0.5 * gain[...]

    def activate(k):
        spot = rows_of(k, block, 2)
        pre = jnp.dot(agg[spot, :], matrix, preferred_element_type=f32) + shift
        sig = 0.5 * jnp.tanh(0.5 * pre) + 0.5
        curve[spot, :] = sig * (1.0 + pre * (1.0 - sig)) * (2.0 / NORM)
        value = (pre * sig).astype(bf16)
        z[spot, :] = value
        turned[:, spot] = value.T
        return value

    for k in range(0, own, 2):
        value = activate(k)
        scaled[rows_of(k, block, 2), :] = (value.astype(f32) * half_gain).astype(bf16)

    def score(k, ib):
        logits = lax.dot_general(
            scaled[rows_of(k, block, 2), :], turned[:, rows_of(ib, block, 2)], (((1,), (0,)), ((), ())),
            preferred_element_type=f32,
        )
        for q in range(2):
            for r in range(2):
                slope[rows_of(k + q, block), rows_of(ib + r, block)] = slope_tile(
                    logits[q * block : (q + 1) * block, r * block : (r + 1) * block],
                    marks[ib + r, rows_of(k + q, block // 2), :],
                    live[pl.ds((ib + r) * own + k + q, 1), :],
                )

    mine = pl.ds(0, own * block)
    for k in range(0, own, 2):
        for ib in range(0, own, 2):
            score(k, ib)
        first_acc[rows_of(k, block, 2), :] = jnp.dot(
            slope[rows_of(k, block, 2), mine], z[mine, :], preferred_element_type=f32
        )

    def second_of(ib):
        return lax.dot_general(
            slope[:, rows_of(ib, block, 2)], scaled[...], (((0,), (0,)), ((), ())), preferred_element_type=f32
        )

    for ib in range(0, own, 2):
        second_acc[rows_of(ib, block, 2), :] = second_of(ib)

    for jj in range(wanted):
        when_from(jj, lambda jj=jj: agg_copy(0, jj).wait_recv())
    for c in range(slot_count):
        when_sent(c, lambda c=c: agg_copy(c, j).wait_send())
    across.wait_send()
    near.wait_send()
    relay.wait_send()

    far_bias[...] = jnp.zeros_like(far_bias)

    @pl.loop(0, wanted // 2)
    def _(step):
        ib = own + 2 * step
        spot = rows_of(ib, block, 2)
        arrived = landed[pl.ds(2 * step, 2)].reshape(2 * block, width)
        agg[spot, :] = arrived
        agg_turned[:, spot] = arrived.T
        value = activate(ib)
        for k in range(0, own, 2):
            score(k, ib)
            first_acc[rows_of(k, block, 2), :] += jnp.dot(
                slope[rows_of(k, block, 2), spot], value, preferred_element_type=f32
            )
        change = second_of(ib) * curve[spot, :]
        dpre[spot, :] = change.astype(bf16)
        far_bias[...] += jnp.sum(change, axis=0, keepdims=True)

    bias_sum = far_bias[...]
    gain_sum = jnp.zeros((1, width), f32)
    for k in range(0, own, 2):
        spot = rows_of(k, block, 2)
        value = first_acc[spot, :]
        gain_sum += jnp.sum(z[spot, :].astype(f32) * value, axis=0, keepdims=True)
        value = (half_gain * value + second_acc[spot, :]) * curve[spot, :]
        bias_sum += jnp.sum(value, axis=0, keepdims=True)
        dpre[spot, :] = value.astype(bf16)
    gain_sum = gain_sum * (1.0 / NORM)
    row = lax.broadcasted_iota(jnp.int32, (EXTRA, width), 0)
    extra = jnp.where(row == 0, bias_sum, jnp.where(row == 1, gain_sum, 0.0))
    extras[...] = extra

    side = width // 2
    piece = side // depth

    def remote(source, target, send, recv, peer):
        return pltpu.make_async_remote_copy(
            src_ref=source, dst_ref=target, send_sem=send, recv_sem=recv, device_id=peer, device_id_type=MESH
        )

    def core_copy(h):
        return remote(part.at[h, 1 - low], recv_core.at[h], core_send.at[h], core_recv.at[h], {"tp": core_peer})

    plane_peers = (d, y_peer), (x_peer, y_peer), (x_peer, t)

    def plane_copy(k):
        return remote(leave.at[k], arrive.at[k], plane_send.at[k], plane_recv.at[k], plane_peers[k])

    def pack_plane(k, h, x, edge):
        edge_high = edge.astype(bf16).astype(f32)
        leave[k, pl.ds(0, 2 * EXTRA), :] = jnp.concatenate([edge_high, edge - edge_high], axis=0).astype(bf16)
        leave[k, pl.ds(2 * EXTRA, side), :] = (
            part[h, low, side_rows(x), :] + recv_core[h, side_rows(x), :]
        ).astype(bf16)
        plane_copy(k).start()

    def z_copy(o):
        p = lax.rem(zi + o, depth)
        return remote(half.at[p], recv_z.at[o], z_send.at[o], z_recv.at[o], {"dom": z_peer(o)})

    here = pl.ds(pl.multiple_of(EXTRA + xi * side + zi * piece, 8), piece)

    def g_copy(o):
        peer = {"dom": lax.rem(d + o, doms)}
        return remote(result.at[here], result.at[here], g_send.at[o], g_recv.at[o], peer)

    def side_rows(x, p=0, many=side):
        return pl.ds(pl.multiple_of(EXTRA + x * side + p * piece, 8), many)

    for h in range(2):
        plane = 1 - high if h == 0 else high
        cut = lambda c, many: pl.ds(pl.multiple_of((plane * 2 + c) * quarter, quarter), many)
        both = jnp.dot(agg_turned[...], dpre[:, cut(0, 2 * quarter)], preferred_element_type=f32)
        for c in range(2):
            part[h, c, pl.ds(EXTRA, width), :] = both[:, c * quarter : (c + 1) * quarter]
            part[h, c, pl.ds(0, EXTRA), :] = extras[:, cut(c, quarter)]
        core_copy(h).start()

    core_copy(0).wait_recv()
    edge = part[0, low, pl.ds(0, EXTRA), :] + recv_core[0, pl.ds(0, EXTRA), :]
    pack_plane(1, 0, 1 - xi, edge)
    pack_plane(0, 0, xi, edge)
    core_copy(1).wait_recv()
    edge = part[1, low, pl.ds(0, EXTRA), :] + recv_core[1, pl.ds(0, EXTRA), :]
    pack_plane(2, 1, 1 - xi, edge)
    for k in range(3):
        plane_copy(k).wait_recv()
    for k in range(3):
        edge_both = arrive[k, pl.ds(0, 2 * EXTRA), :].astype(f32)
        edge += edge_both[:EXTRA] + edge_both[EXTRA:]
    for p in range(depth):
        half[p, pl.ds(0, EXTRA), :] = edge
    for p in range(0, depth, 2):
        sums = part[1, low, side_rows(xi, p, 2 * piece), :] + recv_core[1, side_rows(xi, p, 2 * piece), :]
        for k in range(3):
            sums += arrive[k, pl.ds(2 * EXTRA + p * piece, 2 * piece), :].astype(f32)
        for q in range(2):
            half[p + q, pl.ds(EXTRA, piece), :] = sums[q * piece : (q + 1) * piece]

    @pl.loop(1, depth)
    def _(o):
        z_copy(o).start()

    @pl.loop(1, depth)
    def _(o):
        z_copy(o).wait_recv()

    sums = half[zi]
    for o in range(1, depth):
        sums += recv_z[o]
    result[here, :] = sums[EXTRA:]

    @pl.loop(1, doms)
    def _(o):
        g_copy(o).start()

    result[pl.ds(0, EXTRA), :] = sums[:EXTRA]
    for k in range(2):
        core_copy(k).wait_send()
    for k in range(3):
        plane_copy(k).wait_send()

    @pl.loop(1, depth)
    def _(o):
        z_copy(o).wait_send()

    @pl.loop(1, doms)
    def _(o):
        g_copy(o).wait()


def step(cfg, requests, feat, adj, mask, token, weight, bias, gain, first, second, count, words):
    doms, own, wanted, lanes, slot_count = cfg
    nblocks, block, width = feat.shape
    quarter = weight.shape[1]
    total = own + wanted
    depth = doms // 2
    side = width // 2
    dma = pltpu.SemaphoreType.DMA
    anywhere = pl.BlockSpec(memory_space=pltpu.HBM)
    return pl.pallas_call(
        functools.partial(step_kernel, cfg),
        in_specs=[pl.BlockSpec(memory_space=pltpu.SMEM)] + [anywhere] * 11,
        out_specs=pl.BlockSpec(memory_space=pltpu.VMEM),
        out_shape=jax.ShapeDtypeStruct((EXTRA + width, quarter), f32),
        scratch_shapes=[
            pltpu.VMEM(feat.shape, bf16),
            pltpu.VMEM(adj.shape, bf16),
            pltpu.VMEM(mask.shape, jnp.int32),
            pltpu.VMEM(token.shape, bf16),
            pltpu.VMEM(bias.shape, bf16),
            pltpu.VMEM(gain.shape, f32),
            pltpu.VMEM(first.shape, jnp.int32),
            pltpu.VMEM(second.shape, jnp.int32),
            pltpu.VMEM(count.shape, jnp.int32),
            pltpu.VMEM(words.shape, jnp.int32),
            pltpu.VMEM((width + 16, width), bf16),
            pltpu.VMEM((width + 16, quarter), bf16),
            pltpu.VMEM((slot_count, block, width), bf16),
            pltpu.VMEM((wanted, block, width), bf16),
            pltpu.VMEM((total * block, width), bf16),
            pltpu.VMEM((width, total * block), bf16),
            pltpu.VMEM((total * block, width), bf16),
            pltpu.VMEM((width, total * block), bf16),
            pltpu.VMEM((own * block, width), bf16),
            pltpu.VMEM((total * block, width), f32),
            pltpu.VMEM((total, own * block // 2, block), f32),
            pltpu.VMEM((total * own, block), f32),
            pltpu.VMEM((own * block, total * block), bf16),
            pltpu.VMEM((own * block, width), f32),
            pltpu.VMEM((own * block, width), f32),
            pltpu.VMEM((total * block, width), bf16),
            pltpu.VMEM((2, 2, EXTRA + width, quarter), f32),
            pltpu.VMEM((2, EXTRA + width, quarter), f32),
            pltpu.VMEM((3, 2 * EXTRA + side, quarter), bf16),
            pltpu.VMEM((3, 2 * EXTRA + side, quarter), bf16),
            pltpu.VMEM((depth, EXTRA + side // depth, quarter), f32),
            pltpu.VMEM((depth, EXTRA + side // depth, quarter), f32),
            pltpu.VMEM((1, width), f32),
            pltpu.VMEM((EXTRA, width), f32),
            dma((9 + 3 * lanes,)), dma((3,)), dma((3,)), dma((slot_count,)), dma((wanted,)),
            dma((2,)), dma((2,)), dma((3,)), dma((3,)),
            dma((depth,)), dma((depth,)), dma((doms,)), dma((doms,)),
        ],
        compiler_params=pltpu.CompilerParams(collective_id=0, has_side_effects=True, vmem_limit_bytes=LIMIT),
    )(requests, feat, adj, mask, token, weight, bias, gain, first, second, count, words)


def emit_kernel(result, weight_out, bias_out, gain_out, sem):
    copy = pltpu.make_async_copy(result.at[pl.ds(EXTRA, weight_out.shape[0])], weight_out, sem)
    copy.start()
    bias_out[...] = result[0:1, :]
    gain_out[...] = result[1:2, :]
    copy.wait()


def emit(result):
    tall, quarter = result.shape
    vmem = pl.BlockSpec(memory_space=pltpu.VMEM)
    row = jax.ShapeDtypeStruct((1, quarter), f32)
    return pl.pallas_call(
        emit_kernel,
        in_specs=[vmem],
        out_specs=[pl.BlockSpec(memory_space=pltpu.HBM), vmem, vmem],
        out_shape=(jax.ShapeDtypeStruct((tall - EXTRA, quarter), f32), row, row),
        scratch_shapes=[pltpu.SemaphoreType.DMA],
        compiler_params=pltpu.CompilerParams(vmem_limit_bytes=2 * 1024 * 1024),
    )(result)


def body(
    features, adjacency, node_mask, mask_token, enc_weight, enc_bias, gain, requests,
    pair_first, pair_second, label_words, pair_count,
):
    nodes, width = features.shape
    block = adjacency.shape[1]
    nblocks = nodes // block
    doms = lax.axis_size("dom")
    lanes = lax.axis_size("tp")
    slots = pair_first.shape[2]
    wanted = doms // lanes
    cfg = doms, nblocks // lanes, wanted, lanes, 3 if (doms, lanes) == (8, 4) else wanted
    result = step(
        cfg, requests.reshape(doms),
        features.reshape(nblocks, block, width),
        adjacency.reshape(nblocks, block, block),
        node_mask.reshape(nblocks, 1, block),
        mask_token.reshape(width // 128, 128), enc_weight, enc_bias.reshape(1, -1), gain.reshape(1, width),
        pair_first.reshape(1, slots), pair_second.reshape(1, slots), pair_count.reshape(1, 1),
        label_words.reshape(slots * label_words.shape[3], block),
    )
    weight_grad, bias_grad, gain_grad = emit(result)
    return weight_grad, bias_grad.reshape(-1), gain_grad.reshape(-1)


def solution(mesh):
    placed = (
        P("dom", None),
        P("dom", None),
        P("dom"),
        P(),
        P(None, "tp"),
        P("tp"),
        P(),
        P(None, "dom"),
        P("dom", "tp", None),
        P("dom", "tp", None),
        P("dom", "tp", None, None, None),
        P("dom", "tp"),
    )
    return jax.shard_map(
        body,
        mesh=mesh,
        in_specs=placed,
        out_specs=(P(None, "tp"), P("tp"), P("tp")),
        check_vma=False,
    )
```

```python
import functools

import jax
import jax.numpy as jnp
from jax import lax
from jax.experimental import pallas as pl
from jax.experimental.pallas import tpu as pltpu
from jax.sharding import PartitionSpec as P

NORM = 256.0
WORD = 16
PACK = 256.0
EXTRA = 8
MESH = pl.DeviceIdType.MESH
LIMIT = 60 * 1024 * 1024
f32 = jnp.float32
bf16 = jnp.bfloat16


def served(lane):
    return lax.rem(lane, 2) * 2 + lax.div(lane, 2)


def slope_tile(half_logits, packed_counts, half_live):
    upper = jnp.floor(packed_counts * (1.0 / PACK))
    lower = packed_counts - PACK * upper
    counts = jnp.concatenate(
        [half[k : k + 8] for k in range(0, packed_counts.shape[0], 8) for half in (lower, upper)], axis=0
    )
    return (half_live * jnp.tanh(half_logits) + (half_live - counts)).astype(bf16)


def rows_of(k, block, many=1):
    start = k * block
    if not isinstance(start, int):
        start = pl.multiple_of(start, block)
    return pl.ds(start, many * block)


def step_kernel(
    cfg, requests, feat_hbm, adj_hbm, mask_hbm, token_hbm, weight_hbm, bias_hbm, gain_hbm,
    first_hbm, second_hbm, count_hbm, words_hbm,
    result,
    feat, adj, mask, token, bias, gain, first, second, count, words,
    gathered, packed, asked, landed, agg, agg_turned, z, turned, scaled, curve, marks, live, slope, first_acc, second_acc, dpre,
    part, recv_core, leave, arrive, half, recv_z, far_bias, extras,
    feat_sem, w_send, w_recv, a_send, a_recv, core_send, core_recv, plane_send, plane_recv,
    z_send, z_recv, g_send, g_recv,
):
    doms, own, wanted, lanes, slot_count = cfg
    depth = doms // 2
    d = lax.axis_index("dom")
    t = lax.axis_index("tp")
    low = lax.rem(t, 2)
    high = lax.div(t, 2)
    core_peer = high * 2 + (1 - low)
    y_peer = (1 - high) * 2 + low
    xi = lax.rem(d, 2)
    zi = lax.div(d, 2)
    x_peer = zi * 2 + (1 - xi)
    a = lax.div(d, wanted)
    j = lax.rem(d, wanted)
    width, quarter = weight_hbm.shape
    block = mask.shape[2]

    def z_peer(o):
        return lax.rem(zi + o, depth) * 2 + xi

    pairs = (
        (weight_hbm, packed.at[pl.ds(0, width)]), (bias_hbm, bias), (token_hbm, token), (mask_hbm, mask),
        (gain_hbm, gain), (first_hbm, first), (second_hbm, second), (count_hbm, count),
    )
    for o in range(lanes):
        group = lax.rem(t + o, lanes) * own
        span = pl.ds(group, own)
        pairs += ((adj_hbm.at[span], adj.at[span]),)
        for part_of in range(0, own, own // 2):
            span = pl.ds(group + part_of, own // 2)
            pairs += ((feat_hbm.at[span], feat.at[span]),)
        if o == 0:
            early_fetches = len(pairs)
    pairs += ((words_hbm, words),)
    fetches = [pltpu.make_async_copy(source, target, feat_sem.at[k]) for k, (source, target) in enumerate(pairs)]
    for fetch in fetches:
        fetch.start()

    barrier = pltpu.get_barrier_semaphore()

    def greet(peer):
        pl.semaphore_signal(barrier, inc=1, device_id=peer, device_id_type=MESH)

    greet({"tp": core_peer})
    greet({"tp": y_peer})

    @pl.loop(1, doms)
    def _(o):
        greet({"dom": lax.rem(d + o, doms)})

    greet((x_peer, y_peer))

    if slot_count == 3:
        home = high == lax.div(zi, 2)
        near_z = 2 * lax.div(zi, 2) + low
        far_z = 2 * (1 - lax.div(zi, 2)) + low
        outgoing = (
            (None, far_z * 2 + jnp.where(home, xi, 1 - xi)),
            (home, near_z * 2 + xi),
            (home, near_z * 2 + 1 - xi),
        )
        mine_slot = 1
        alone = zi == t

        def lane_from(jj):
            same_half = lax.div(zi, 2) == high
            straight = jnp.logical_or(same_half, xi == jj)
            return jnp.where(straight, high, 1 - high) * 2 + lax.rem(zi, 2)

        sends = 1 + jnp.where(home, 2, 0)
    else:
        outgoing = tuple((None, served(t) * wanted + lax.rem(j + c, wanted)) for c in range(wanted))
        mine_slot = 0
        alone = jnp.logical_and(a == t, served(t) == t)

        def lane_from(jj):
            return served(a)

        sends = wanted

    def when_sent(c, do):
        active = outgoing[c][0]
        if c == mine_slot:
            other = jnp.logical_not(alone)
            active = other if active is None else jnp.logical_and(active, other)
        if active is None:
            do()
        else:
            pl.when(active)(do)

    def when_from(jj, do):
        pl.when(jnp.logical_not(jnp.logical_and(alone, j == jj)))(do)

    for c in range(slot_count):
        when_sent(c, functools.partial(greet, (outgoing[c][1], a)))
    for jj in range(wanted):
        when_from(jj, functools.partial(greet, (t * wanted + jj, lane_from(jj))))

    columns = lambda c: pl.ds(pl.multiple_of(c * quarter, quarter), quarter)
    fetches[0].wait()
    fetches[1].wait()
    packed[pl.ds(width, 16), :] = jnp.broadcast_to(bias[...], (16, quarter))
    gathered[:, columns(t)] = packed[...]
    pl.semaphore_wait(barrier, 2 + doms + wanted + sends - jnp.where(alone, 2, 0))

    def weight_copy(k, source, column, peer):
        return pltpu.make_async_remote_copy(
            src_ref=source, dst_ref=gathered.at[:, columns(column)],
            send_sem=w_send.at[k], recv_sem=w_recv.at[k],
            device_id={"tp": peer}, device_id_type=MESH,
        )

    across = weight_copy(0, packed, t, y_peer)
    near = weight_copy(1, packed, t, core_peer)
    relay = weight_copy(2, gathered.at[:, columns(y_peer)], y_peer, core_peer)
    across.start()
    near.start()

    rows = lax.broadcasted_iota(jnp.int32, (block, block), 0)
    cols = lax.broadcasted_iota(jnp.int32, (block, block), 1)
    for fetch in fetches[2:early_fetches]:
        fetch.wait()
    token32 = token[...].astype(f32)
    token_row = jnp.concatenate([token32[k : k + 1, :] for k in range(token32.shape[0])], axis=1)

    def aggregate(node_block):
        hidden = jnp.sum(jnp.where(rows == cols, mask[node_block].astype(f32), 0.0), axis=1, keepdims=True)
        masked32 = jnp.where(hidden == 1.0, token_row, feat[node_block].astype(f32))
        mixed = jnp.dot(adj[node_block], masked32.astype(bf16), preferred_element_type=f32)
        return (masked32 + mixed).astype(bf16)

    for k in range(own):
        value = aggregate(t * own + k)
        agg[rows_of(k, block), :] = value
        agg_turned[:, rows_of(k, block)] = value.T

    for fetch in fetches[early_fetches:]:
        fetch.wait()

    def agg_copy(c, slot):
        return pltpu.make_async_remote_copy(
            src_ref=asked.at[c], dst_ref=landed.at[slot],
            send_sem=a_send.at[c], recv_sem=a_recv.at[slot],
            device_id=(outgoing[c][1], a), device_id_type=MESH,
        )

    for c in range(slot_count):
        asked[c] = aggregate(requests[outgoing[c][1]])
        if slot_count == 3 and c == 0:
            pl.when(home)(lambda: agg_copy(0, j).start())
        else:
            when_sent(c, lambda c=c: agg_copy(c, j).start())

    @pl.when(alone)
    def _():
        landed[j] = asked[mine_slot]

    slots = first.shape[1]
    cells = own * (own + wanted)
    key = second[...] * own + first[...]
    cell = lax.broadcasted_iota(jnp.int32, (cells, slots), 0)
    slot = lax.broadcasted_iota(jnp.int32, (cells, slots), 1)
    hot32 = jnp.where(jnp.logical_and(cell == key, slot < count[...]), 1.0, 0.0)
    live[...] = jnp.broadcast_to(0.5 * jnp.sum(hot32, axis=1, keepdims=True), (cells, block))
    hot = jnp.concatenate([hot32, PACK * hot32], axis=1).astype(bf16)

    def count_labels(w):
        word = words[pl.ds(w, slots, stride=block // WORD), :]

        def bit(b):
            return jnp.where(jnp.bitwise_and(word, 1 << b) == 0, 0.0, 1.0).astype(bf16)

        for b in range(0, WORD // 2, 2):
            bits = jnp.concatenate(
                [jnp.concatenate([bit(b + q), bit(b + q + WORD // 2)], axis=0) for q in range(2)], axis=1
            )
            counts = jnp.dot(hot, bits, preferred_element_type=f32)
            for q in range(2):
                for ib in range(own + wanted):
                    marks[ib, pl.ds(w * (WORD // 2) + b + q, own, stride=block // 2), :] = counts[
                        ib * own : (ib + 1) * own, q * block : (q + 1) * block
                    ]

    early = block // WORD // 2
    pl.loop(0, early)(count_labels)
    across.wait_recv()
    relay.start()
    if slot_count == 3:
        pl.when(jnp.logical_not(home))(lambda: agg_copy(0, j).start())
    pl.loop(early, block // WORD)(count_labels)
    near.wait_recv()
    relay.wait_recv()

    matrix = gathered[:width, :]
    shift = gathered[width : width + 1, :].astype(f32)
    half_gain = 0.5 * gain[...]

    def activate(k):
        spot = rows_of(k, block, 2)
        pre = jnp.dot(agg[spot, :], matrix, preferred_element_type=f32) + shift
        sig = 0.5 * jnp.tanh(0.5 * pre) + 0.5
        curve[spot, :] = sig * (1.0 + pre * (1.0 - sig)) * (2.0 / NORM)
        value = (pre * sig).astype(bf16)
        z[spot, :] = value
        turned[:, spot] = value.T
        return value

    for k in range(0, own, 2):
        value = activate(k)
        scaled[rows_of(k, block, 2), :] = (value.astype(f32) * half_gain).astype(bf16)

    def score(k, ib):
        logits = lax.dot_general(
            scaled[rows_of(k, block, 2), :], turned[:, rows_of(ib, block, 2)], (((1,), (0,)), ((), ())),
            preferred_element_type=f32,
        )
        for q in range(2):
            for r in range(2):
                slope[rows_of(k + q, block), rows_of(ib + r, block)] = slope_tile(
                    logits[q * block : (q + 1) * block, r * block : (r + 1) * block],
                    marks[ib + r, rows_of(k + q, block // 2), :],
                    live[pl.ds((ib + r) * own + k + q, 1), :],
                )

    mine = pl.ds(0, own * block)
    for k in range(0, own, 2):
        for ib in range(0, own, 2):
            score(k, ib)
        first_acc[rows_of(k, block, 2), :] = jnp.dot(
            slope[rows_of(k, block, 2), mine], z[mine, :], preferred_element_type=f32
        )

    def second_of(ib):
        return lax.dot_general(
            slope[:, rows_of(ib, block, 2)], scaled[...], (((0,), (0,)), ((), ())), preferred_element_type=f32
        )

    for ib in range(0, own, 2):
        second_acc[rows_of(ib, block, 2), :] = second_of(ib)

    for jj in range(wanted):
        when_from(jj, lambda jj=jj: agg_copy(0, jj).wait_recv())
    for c in range(slot_count):
        when_sent(c, lambda c=c: agg_copy(c, j).wait_send())
    across.wait_send()
    near.wait_send()
    relay.wait_send()

    far_bias[...] = jnp.zeros_like(far_bias)

    @pl.loop(0, wanted // 2)
    def _(step):
        ib = own + 2 * step
        spot = rows_of(ib, block, 2)
        arrived = landed[pl.ds(2 * step, 2)].reshape(2 * block, width)
        agg[spot, :] = arrived
        agg_turned[:, spot] = arrived.T
        value = activate(ib)
        for k in range(0, own, 2):
            score(k, ib)
            first_acc[rows_of(k, block, 2), :] += jnp.dot(
                slope[rows_of(k, block, 2), spot], value, preferred_element_type=f32
            )
        change = second_of(ib) * curve[spot, :]
        dpre[spot, :] = change.astype(bf16)
        far_bias[...] += jnp.sum(change, axis=0, keepdims=True)

    bias_sum = far_bias[...]
    gain_sum = jnp.zeros((1, width), f32)
    for k in range(0, own, 2):
        spot = rows_of(k, block, 2)
        value = first_acc[spot, :]
        gain_sum += jnp.sum(z[spot, :].astype(f32) * value, axis=0, keepdims=True)
        value = (half_gain * value + second_acc[spot, :]) * curve[spot, :]
        bias_sum += jnp.sum(value, axis=0, keepdims=True)
        dpre[spot, :] = value.astype(bf16)
    gain_sum = gain_sum * (1.0 / NORM)
    row = lax.broadcasted_iota(jnp.int32, (EXTRA, width), 0)
    extra = jnp.where(row == 0, bias_sum, jnp.where(row == 1, gain_sum, 0.0))
    extras[...] = extra

    side = width // 2
    piece = side // depth

    def remote(source, target, send, recv, peer):
        return pltpu.make_async_remote_copy(
            src_ref=source, dst_ref=target, send_sem=send, recv_sem=recv, device_id=peer, device_id_type=MESH
        )

    def core_copy(h):
        return remote(part.at[h, 1 - low], recv_core.at[h], core_send.at[h], core_recv.at[h], {"tp": core_peer})

    plane_peers = (d, y_peer), (x_peer, y_peer), (x_peer, t)

    def plane_copy(k):
        return remote(leave.at[k], arrive.at[k], plane_send.at[k], plane_recv.at[k], plane_peers[k])

    def pack_plane(k, h, x, edge):
        edge_high = edge.astype(bf16).astype(f32)
        leave[k, pl.ds(0, 2 * EXTRA), :] = jnp.concatenate([edge_high, edge - edge_high], axis=0).astype(bf16)
        leave[k, pl.ds(2 * EXTRA, side), :] = (
            part[h, low, side_rows(x), :] + recv_core[h, side_rows(x), :]
        ).astype(bf16)
        plane_copy(k).start()

    def z_copy(o):
        p = lax.rem(zi + o, depth)
        return remote(half.at[p], recv_z.at[o], z_send.at[o], z_recv.at[o], {"dom": z_peer(o)})

    here = pl.ds(pl.multiple_of(EXTRA + xi * side + zi * piece, 8), piece)

    def g_copy(o):
        peer = {"dom": lax.rem(d + o, doms)}
        return remote(result.at[here], result.at[here], g_send.at[o], g_recv.at[o], peer)

    def side_rows(x, p=0, many=side):
        return pl.ds(pl.multiple_of(EXTRA + x * side + p * piece, 8), many)

    for h in range(2):
        plane = 1 - high if h == 0 else high
        cut = lambda c, many: pl.ds(pl.multiple_of((plane * 2 + c) * quarter, quarter), many)
        both = jnp.dot(agg_turned[...], dpre[:, cut(0, 2 * quarter)], preferred_element_type=f32)
        for c in range(2):
            part[h, c, pl.ds(EXTRA, width), :] = both[:, c * quarter : (c + 1) * quarter]
            part[h, c, pl.ds(0, EXTRA), :] = extras[:, cut(c, quarter)]
        core_copy(h).start()

    core_copy(0).wait_recv()
    edge = part[0, low, pl.ds(0, EXTRA), :] + recv_core[0, pl.ds(0, EXTRA), :]
    pack_plane(1, 0, 1 - xi, edge)
    pack_plane(0, 0, xi, edge)
    core_copy(1).wait_recv()
    edge = part[1, low, pl.ds(0, EXTRA), :] + recv_core[1, pl.ds(0, EXTRA), :]
    pack_plane(2, 1, 1 - xi, edge)
    for k in range(3):
        plane_copy(k).wait_recv()
    for k in range(3):
        edge_both = arrive[k, pl.ds(0, 2 * EXTRA), :].astype(f32)
        edge += edge_both[:EXTRA] + edge_both[EXTRA:]
    for p in range(depth):
        half[p, pl.ds(0, EXTRA), :] = edge
    for p in range(0, depth, 2):
        sums = part[1, low, side_rows(xi, p, 2 * piece), :] + recv_core[1, side_rows(xi, p, 2 * piece), :]
        for k in range(3):
            sums += arrive[k, pl.ds(2 * EXTRA + p * piece, 2 * piece), :].astype(f32)
        for q in range(2):
            half[p + q, pl.ds(EXTRA, piece), :] = sums[q * piece : (q + 1) * piece]

    @pl.loop(0, depth - 1)
    def _(o):
        z_copy(1 + lax.rem(o + depth // 2 - 1, depth - 1)).start()

    @pl.loop(1, depth)
    def _(o):
        z_copy(o).wait_recv()

    sums = half[zi]
    for o in range(1, depth):
        sums += recv_z[o]
    result[here, :] = sums[EXTRA:]

    @pl.loop(0, doms - 1)
    def _(o):
        g_copy(1 + lax.rem(o + doms // 2 - 2, doms - 1)).start()

    result[pl.ds(0, EXTRA), :] = sums[:EXTRA]
    for k in range(2):
        core_copy(k).wait_send()
    for k in range(3):
        plane_copy(k).wait_send()

    @pl.loop(1, depth)
    def _(o):
        z_copy(o).wait_send()

    @pl.loop(1, doms)
    def _(o):
        g_copy(o).wait()


def step(cfg, requests, feat, adj, mask, token, weight, bias, gain, first, second, count, words):
    doms, own, wanted, lanes, slot_count = cfg
    nblocks, block, width = feat.shape
    quarter = weight.shape[1]
    total = own + wanted
    depth = doms // 2
    side = width // 2
    dma = pltpu.SemaphoreType.DMA
    anywhere = pl.BlockSpec(memory_space=pltpu.HBM)
    return pl.pallas_call(
        functools.partial(step_kernel, cfg),
        in_specs=[pl.BlockSpec(memory_space=pltpu.SMEM)] + [anywhere] * 11,
        out_specs=pl.BlockSpec(memory_space=pltpu.VMEM),
        out_shape=jax.ShapeDtypeStruct((EXTRA + width, quarter), f32),
        scratch_shapes=[
            pltpu.VMEM(feat.shape, bf16),
            pltpu.VMEM(adj.shape, bf16),
            pltpu.VMEM(mask.shape, jnp.int32),
            pltpu.VMEM(token.shape, bf16),
            pltpu.VMEM(bias.shape, bf16),
            pltpu.VMEM(gain.shape, f32),
            pltpu.VMEM(first.shape, jnp.int32),
            pltpu.VMEM(second.shape, jnp.int32),
            pltpu.VMEM(count.shape, jnp.int32),
            pltpu.VMEM(words.shape, jnp.int32),
            pltpu.VMEM((width + 16, width), bf16),
            pltpu.VMEM((width + 16, quarter), bf16),
            pltpu.VMEM((slot_count, block, width), bf16),
            pltpu.VMEM((wanted, block, width), bf16),
            pltpu.VMEM((total * block, width), bf16),
            pltpu.VMEM((width, total * block), bf16),
            pltpu.VMEM((total * block, width), bf16),
            pltpu.VMEM((width, total * block), bf16),
            pltpu.VMEM((own * block, width), bf16),
            pltpu.VMEM((total * block, width), f32),
            pltpu.VMEM((total, own * block // 2, block), f32),
            pltpu.VMEM((total * own, block), f32),
            pltpu.VMEM((own * block, total * block), bf16),
            pltpu.VMEM((own * block, width), f32),
            pltpu.VMEM((own * block, width), f32),
            pltpu.VMEM((total * block, width), bf16),
            pltpu.VMEM((2, 2, EXTRA + width, quarter), f32),
            pltpu.VMEM((2, EXTRA + width, quarter), f32),
            pltpu.VMEM((3, 2 * EXTRA + side, quarter), bf16),
            pltpu.VMEM((3, 2 * EXTRA + side, quarter), bf16),
            pltpu.VMEM((depth, EXTRA + side // depth, quarter), f32),
            pltpu.VMEM((depth, EXTRA + side // depth, quarter), f32),
            pltpu.VMEM((1, width), f32),
            pltpu.VMEM((EXTRA, width), f32),
            dma((9 + 3 * lanes,)), dma((3,)), dma((3,)), dma((slot_count,)), dma((wanted,)),
            dma((2,)), dma((2,)), dma((3,)), dma((3,)),
            dma((depth,)), dma((depth,)), dma((doms,)), dma((doms,)),
        ],
        compiler_params=pltpu.CompilerParams(collective_id=0, has_side_effects=True, vmem_limit_bytes=LIMIT),
    )(requests, feat, adj, mask, token, weight, bias, gain, first, second, count, words)


def emit_kernel(result, weight_out, bias_out, gain_out, sem):
    copy = pltpu.make_async_copy(result.at[pl.ds(EXTRA, weight_out.shape[0])], weight_out, sem)
    copy.start()
    bias_out[...] = result[0:1, :]
    gain_out[...] = result[1:2, :]
    copy.wait()


def emit(result):
    tall, quarter = result.shape
    vmem = pl.BlockSpec(memory_space=pltpu.VMEM)
    row = jax.ShapeDtypeStruct((1, quarter), f32)
    return pl.pallas_call(
        emit_kernel,
        in_specs=[vmem],
        out_specs=[pl.BlockSpec(memory_space=pltpu.HBM), vmem, vmem],
        out_shape=(jax.ShapeDtypeStruct((tall - EXTRA, quarter), f32), row, row),
        scratch_shapes=[pltpu.SemaphoreType.DMA],
        compiler_params=pltpu.CompilerParams(vmem_limit_bytes=2 * 1024 * 1024),
    )(result)


def body(
    features, adjacency, node_mask, mask_token, enc_weight, enc_bias, gain, requests,
    pair_first, pair_second, label_words, pair_count,
):
    nodes, width = features.shape
    block = adjacency.shape[1]
    nblocks = nodes // block
    doms = lax.axis_size("dom")
    lanes = lax.axis_size("tp")
    slots = pair_first.shape[2]
    wanted = doms // lanes
    cfg = doms, nblocks // lanes, wanted, lanes, 3 if (doms, lanes) == (8, 4) else wanted
    result = step(
        cfg, requests.reshape(doms),
        features.reshape(nblocks, block, width),
        adjacency.reshape(nblocks, block, block),
        node_mask.reshape(nblocks, 1, block),
        mask_token.reshape(width // 128, 128), enc_weight, enc_bias.reshape(1, -1), gain.reshape(1, width),
        pair_first.reshape(1, slots), pair_second.reshape(1, slots), pair_count.reshape(1, 1),
        label_words.reshape(slots * label_words.shape[3], block),
    )
    weight_grad, bias_grad, gain_grad = emit(result)
    return weight_grad, bias_grad.reshape(-1), gain_grad.reshape(-1)


def solution(mesh):
    placed = (
        P("dom", None),
        P("dom", None),
        P("dom"),
        P(),
        P(None, "tp"),
        P("tp"),
        P(),
        P(None, "dom"),
        P("dom", "tp", None),
        P("dom", "tp", None),
        P("dom", "tp", None, None, None),
        P("dom", "tp"),
    )
    return jax.shard_map(
        body,
        mesh=mesh,
        in_specs=placed,
        out_specs=(P(None, "tp"), P("tp"), P("tp")),
        check_vma=False,
    )
```
